256 devices in a mesh: pipe: 2 (over core), group: 16 (over x, y), local: 8 (over z).
Axes of the slice: x: 4, y: 4, z: 8, core: 2. Of those that a mesh axis runs over, the one named last changes fastest.
Arguments:
- output_grad: bfloat16 [2, 4096, 2048], P(None, ('group', 'local')), may hold values from -6 to 6
- carried_grad: bfloat16 [4096, 2048], P(('group', 'local')), may hold values from -6 to 6
- layer_inputs: bfloat16 [2, 2, 4096, 2048], P('pipe', None, ('group', 'local')), may hold values from -6 to 6
- expert_ids: int32 [2, 2, 4096, 6], P('pipe', None, ('group', 'local')), may hold values from 0 to 63, all different within a row; in each aligned block of 32 rows (0 to 31, 32 to 63, ..., all dimensions but the last counted through in order) at most 4 rows name the same one
- gate_prob: bfloat16 [2, 2, 4096, 6], P('pipe', None, ('group', 'local')), may hold values from 0.099609375 to 0.796875
- gate_weight: bfloat16 [2, 128, 2048, 704], P('pipe', ('group', 'local')), may hold values from -0.125 to 0.125
- up_weight: bfloat16 [2, 128, 2048, 704], P('pipe', ('group', 'local')), may hold values from -0.125 to 0.125
- down_weight: bfloat16 [2, 128, 704, 2048], P('pipe', ('group', 'local')), may hold values from -0.15625 to 0.15625
Outputs:
- input_grad: bfloat16 [2, 2, 4096, 2048], P('pipe', None, ('group', 'local'))
- gate_grad: bfloat16 [2, 2, 4096, 6], P('pipe', None, ('group', 'local'))
The draws below stay inside these ranges and needn't reach their ends.
Inputs may be any that keep to these rules, and one draw needn't show every extreme that they name: `expert_ids`: each token names 6 different experts. Within each section and microbatch, the 32 tokens of one device (aligned blocks of rows) name any one expert at most 4 times.
All inputs are finite; a program needn't handle non-finite values.
Results may differ from the reference program's by a relative error of at most 0.0065.
Values may be sent and summed in bfloat16 or wider, within the bound.
A program may use at most 128 MiB of HBM per device.

```python
import math
import jax
import jax.numpy as jnp
import numpy as np
from jax import lax

D = 2048
FF = 1408
TOP = 6
TOK_DEV = 32
MICRO = 2
SECTIONS = 2
EXPERTS = 64
ECAP = 4
TOKENS = 4096


def block_scale(own_key, shape, pieces, least, top_value):
    loudness = 1.0
    for axis_at, parts in pieces:
        draws = jax.random.uniform(jax.random.fold_in(jax.random.fold_in(own_key, 6), axis_at), (parts,), jnp.float32, least / len(pieces), top_value / len(pieces))
        loudness = loudness * jnp.repeat(jnp.exp(draws), shape[axis_at] // parts).reshape((-1,) + (1,) * (len(shape) - 1 - axis_at))
    return loudness


def shared_out(own_key, own, number, rows, amount, top, bound, slope):
    ranking = jax.random.permutation(own_key, amount)
    crowded, usual = shares(amount, rows * top, bound, slope, True), shares(amount, rows * top, bound, slope, False)
    places = jnp.arange(amount)

    def named(sizes, offset_by):
        used = int((sizes > 0).sum())
        fixed = max(1, used // 4)
        shifted = fixed + (places - fixed + offset_by * (used - fixed)) % max(1, amount - fixed)
        return jnp.zeros((amount,), jnp.int32).at[ranking[jnp.where(places < fixed, places, shifted)]].set(jnp.asarray(sizes, jnp.int32))

    sizes = jnp.where(number % 4 == 0, named(crowded, number // 4), named(usual, number - number // 4 - 1))
    mixed = jax.random.permutation(jax.random.fold_in(own, 3), amount)
    giver, receiver = mixed[0:amount // 2 * 2:2], mixed[1:amount // 2 * 2:2]
    room = jnp.minimum(sizes[giver] - 1, bound - sizes[receiver]) // 2
    room = jnp.where((giver == ranking[0]) | (receiver == ranking[0]) | (sizes[receiver] == 0), 0, jnp.maximum(room, 0))
    shifted = jax.random.randint(jax.random.fold_in(own, 4), (amount // 2,), 0, 1 << 20) % (room + 1)
    sizes = sizes.at[giver].add(-shifted).at[receiver].add(shifted)
    labels = jnp.searchsorted(jnp.cumsum(sizes), jnp.arange(rows * top), side="right").astype(jnp.int32)
    table = labels.reshape(top, rows).T
    table = table[jax.random.permutation(jax.random.fold_in(own, 1), rows)]
    offset_by = jax.random.randint(jax.random.fold_in(own, 2), (rows, 1), 0, top)
    return jnp.take_along_axis(table, (jnp.arange(top)[None, :] + offset_by) % top, axis=1)


def shares(number_of, total, bound, slope, full):
    loads = [(1 << 20) // math.isqrt(grade ** slope) + 1 for grade in range(1, number_of + 1)]
    largest = bound if full else min(bound, max(-(-total // number_of), total * loads[0] // sum(loads)))
    least = 1 if total - largest >= number_of - 1 else 0
    given, rest = [largest] + [least] * (number_of - 1), total - largest - least * (number_of - 1)
    while rest > 0:
        free = [i for i in range(1, number_of) if given[i] < largest] or [i for i in range(1, number_of) if given[i] < bound]
        pool, left = sum([loads[i] for i in free]), rest
        for i in free:
            addition = min(bound - given[i], max(1, left * loads[i] // pool), rest)
            given[i] = given[i] + addition
            rest = rest - addition
    return np.array(given)


def noise(stream_key, shape, deviation, limit, shards=(), held_as=jnp.bfloat16):
    level = block_scale(stream_key, shape, shards, -0.22, 0.18) if shards else 1.0
    values = jax.random.normal(stream_key, shape, jnp.float32) * deviation * level
    return jnp.minimum(jnp.maximum(values, -limit), limit).astype(held_as)


def setup_inputs(seed: int = 0) -> dict:
    arg_keys = jax.random.split(jax.random.key(seed), 9)
    output_grad = noise(arg_keys[0], (MICRO, TOKENS, D), 1.0, 6.0, ((1, 128),))
    carried_grad = noise(arg_keys[1], (TOKENS, D), 1.0, 6.0, ((0, 128),))
    layer_inputs = noise(arg_keys[2], (SECTIONS, MICRO, TOKENS, D), 1.0, 6.0, ((0, 2), (2, 128)))
    expert_ids_keys = jax.random.split(jax.random.fold_in(arg_keys[3], 1), SECTIONS * MICRO * TOKENS // TOK_DEV)
    expert_ids_turns = jax.random.permutation(jax.random.fold_in(arg_keys[3], 3), SECTIONS * MICRO * TOKENS // TOK_DEV)
    expert_ids = jax.vmap(lambda own, number: shared_out(jax.random.fold_in(arg_keys[3], 2), own, number, TOK_DEV, EXPERTS, TOP, ECAP, 1))(expert_ids_keys, expert_ids_turns).reshape((SECTIONS, MICRO, TOKENS, TOP))
    gate_prob = jnp.clip(0.099609375 + 0.6972656 * jax.random.uniform(arg_keys[4], (SECTIONS, MICRO, TOKENS, TOP), jnp.float32) ** block_scale(arg_keys[4], (SECTIONS, MICRO, TOKENS, TOP), ((0, 2), (2, 128)), -0.2, 0.2), 0.099609375, 0.796875).astype(jnp.bfloat16)
    gate_weight = noise(arg_keys[5], (SECTIONS, 2 * EXPERTS, D, FF // 2), D ** -0.5, 0.125, ((0, 2), (1, 128)))
    up_weight = noise(arg_keys[6], (SECTIONS, 2 * EXPERTS, D, FF // 2), D ** -0.5, 0.125, ((0, 2), (1, 128)))
    down_weight = noise(arg_keys[7], (SECTIONS, 2 * EXPERTS, FF // 2, D), FF ** -0.5, 0.15625, ((0, 2), (1, 128)))
    return {"output_grad": output_grad, "carried_grad": carried_grad, "layer_inputs": layer_inputs, "expert_ids": expert_ids, "gate_prob": gate_prob, "gate_weight": gate_weight, "up_weight": up_weight, "down_weight": down_weight}


def expert_backward(rows_in, rows_grad, row_probs, gate_full, up_full, down_full):
    rows_in = rows_in.astype(jnp.float32)
    rows_grad = rows_grad.astype(jnp.float32)
    gate_pre = jnp.dot(rows_in, gate_full.astype(jnp.float32))
    up_pre = jnp.dot(rows_in, up_full.astype(jnp.float32))
    back_proj = jnp.dot(rows_grad, down_full.astype(jnp.float32).T)
    sigmoid_gate = jax.nn.sigmoid(gate_pre)
    activated = gate_pre * sigmoid_gate
    gate_part = jnp.sum(activated * up_pre * back_proj, axis=1)
    scaled = row_probs[:, None] * back_proj
    grad_gate = (scaled * up_pre * sigmoid_gate * (1.0 + gate_pre * (1.0 - sigmoid_gate))).astype(jnp.bfloat16)
    grad_up = (scaled * activated).astype(jnp.bfloat16)
    grad_rows = jnp.dot(grad_gate.astype(jnp.float32), gate_full.astype(jnp.float32).T)
    grad_rows = grad_rows + jnp.dot(grad_up.astype(jnp.float32), up_full.astype(jnp.float32).T)
    return grad_rows, gate_part


def reference(output_grad, carried_grad, layer_inputs, expert_ids, gate_prob, gate_weight, up_weight, down_weight):
    def layer_backward(section_index, micro_index, incoming):
        choices_ids = expert_ids[section_index, micro_index]
        inputs = layer_inputs[section_index, micro_index]
        weights_prob = gate_prob[section_index, micro_index].astype(jnp.float32)
        expert_range = jnp.arange(EXPERTS, dtype=jnp.int32)
        matches = (choices_ids[:, :, None] == expert_range[None, None, :]).astype(jnp.int32)
        chosen = jnp.sum(matches, axis=1)
        before = jnp.cumsum(chosen, axis=0) - chosen
        position = jnp.sum(matches * before[:, None, :], axis=2).astype(jnp.int32)
        capacity_rows = (TOKENS // TOK_DEV) * ECAP
        token_index = jnp.broadcast_to(jnp.arange(TOKENS, dtype=jnp.int32)[:, None], choices_ids.shape)
        index_table = jnp.zeros((EXPERTS, capacity_rows), jnp.int32).at[choices_ids, position].set(token_index)
        prob_table = jnp.zeros((EXPERTS, capacity_rows), jnp.float32).at[choices_ids, position].set(weights_prob)
        gate_halves = gate_weight[section_index].reshape(EXPERTS, 2, D, FF // 2)
        up_halves = up_weight[section_index].reshape(EXPERTS, 2, D, FF // 2)
        down_halves = down_weight[section_index].reshape(EXPERTS, 2, FF // 2, D)

        def per_expert(operands):
            index_row, prob_row, gate_pair, up_pair, down_pair = operands
            gate_full = jnp.concatenate([gate_pair[0], gate_pair[1]], axis=1)
            up_full = jnp.concatenate([up_pair[0], up_pair[1]], axis=1)
            down_full = jnp.concatenate([down_pair[0], down_pair[1]], axis=0)
            grad_rows, gate_part = expert_backward(inputs[index_row], incoming[index_row], prob_row, gate_full, up_full, down_full)
            return grad_rows.astype(jnp.bfloat16), gate_part.astype(jnp.bfloat16)

        contrib, gate_parts = lax.map(per_expert, (index_table, prob_table, gate_halves, up_halves, down_halves))
        added = jnp.zeros((TOKENS, D), jnp.float32).at[index_table.reshape(-1)].add(contrib.reshape(-1, D).astype(jnp.float32))
        summed = incoming.astype(jnp.float32) + added
        return summed.astype(jnp.bfloat16), gate_parts[choices_ids, position]

    grads_last = []
    gates_last = []
    for micro_index in range(MICRO):
        result_grad, result_gate = layer_backward(1, micro_index, output_grad[micro_index])
        grads_last.append(result_grad)
        gates_last.append(result_gate)
    grads_first = []
    gates_first = []
    for micro_index in range(MICRO):
        if micro_index == 0:
            incoming = carried_grad
        else:
            incoming = grads_last[micro_index - 1]
        result_grad, result_gate = layer_backward(0, micro_index, incoming)
        grads_first.append(result_grad)
        gates_first.append(result_gate)
    input_grad = jnp.stack([jnp.stack(grads_first), jnp.stack(grads_last)])
    gate_grad = jnp.stack([jnp.stack(gates_first), jnp.stack(gates_last)])
    return input_grad, gate_grad
```

```python
import functools

import jax
import jax.numpy as jnp
from jax import lax
from jax.experimental import pallas as pl
from jax.experimental.pallas import tpu as pltpu
from jax.sharding import PartitionSpec as P

MESH = pl.DeviceIdType.MESH
NX, NY, NZ = 4, 4, 8
NG = NX * NY
TOK, D, HALF, SLOTS = 32, 2048, 704, 4
ROWS = NG * TOK
ALL = NZ * TOK
HALVES = 2
W = D // HALVES
EXTRA = 128
WIDE = (W, W + EXTRA)
STEPS = ((4, 3), (3, 4))
NT = (((1,), (1,)), ((), ()))
F32, BF16 = jnp.float32, jnp.bfloat16


def nt_dot(a, b):
    return lax.dot_general(a, b, NT, preferred_element_type=F32)


def kernel(
    og_ref, cg_ref, xin_ref, ids_ref, pr_ref, wg_hbm, wu_hbm, wd_hbm,
    out_ref, gate_ref,
    wg, wu, wd, meta, own_grad, passed, finished,
    gathered, picked, arrived, sent_back, came_back0, came_back1, sent_wide,
    a_acc, b_acc, q_acc, da_buf, db_buf, dmat, cmat, mmat, p0, p1,
    rs_send, rs_recv,
    w_sem, meta_ss, meta_rs, ag_ss, ag_rs, x_ss, x_rs, r_ss, r_rs, rs_ss, rs_rs, pass_ss, pass_rs,
):
    pipe = lax.axis_index("pipe")
    g = lax.axis_index("group")
    z = lax.axis_index("local")
    x, y = g // NY, g % NY
    up = (pipe, g, lax.rem(z + 1, NZ))
    down = (pipe, g, lax.rem(z + NZ - 1, NZ))
    partner = (1 - pipe, g, z)
    came_back = (came_back0, came_back1)
    back_out = (sent_back, sent_wide)
    sums = (p0, p1)
    waits = []

    def remote(src, dst, ss, rs, device):
        copy = pltpu.make_async_remote_copy(
            src_ref=src, dst_ref=dst, send_sem=ss, recv_sem=rs, device_id=device, device_id_type=MESH
        )
        return copy

    loads = []
    for i, (h, v) in enumerate(((wg_hbm, wg), (wu_hbm, wu), (wd_hbm, wd))):
        copy = pltpu.make_async_copy(h, v, w_sem.at[i])
        copy.start()
        loads.append(copy)

    barrier = pltpu.get_barrier_semaphore()

    def plane_peer(i):
        diag, dx = i // NX, i % NX
        dy = lax.rem(diag - dx + NY, NY)
        return lax.rem(x + dx, NX) * NY + lax.rem(y + dy, NY)

    def greet(i, carry):
        pl.semaphore_signal(barrier, inc=1, device_id=(pipe, plane_peer(i), z), device_id_type=MESH)
        return carry

    for device in (up, down, partner):
        pl.semaphore_signal(barrier, inc=1, device_id=device, device_id_type=MESH)
    lax.fori_loop(1, NG, greet, 0)

    lane = lax.broadcasted_iota(jnp.int32, (TOK, EXTRA), 1)
    lower = (
        lax.broadcasted_iota(jnp.int32, (TOK, TOK), 0) > lax.broadcasted_iota(jnp.int32, (TOK, TOK), 1)
    ).astype(BF16)
    for m in range(2):
        ids = ids_ref[m]
        probs = pr_ref[m].astype(F32)
        chosen = jnp.zeros((TOK, EXTRA), F32)
        weight = jnp.zeros((TOK, EXTRA), F32)
        for k in range(ids.shape[1]):
            chosen += (lane == ids[:, k : k + 1]).astype(F32)
            weight += jnp.where(lane == ids[:, k : k + 1] + 64, probs[:, k : k + 1], 0.0)
        before = jnp.dot(lower, chosen.astype(BF16), preferred_element_type=F32)
        meta[z, m] = (chosen * (before + 1.0) + weight).astype(BF16)
    is_last = pipe == 1
    own_grad[0] = jnp.where(is_last, og_ref[0].astype(F32), cg_ref[...].astype(F32)).astype(BF16)

    pl.semaphore_wait(barrier, NG - 1 + 3)

    def ring_items(first_src, at, ss, rs, counts):
        nr, nl = counts

        def hop(direction, s):
            if direction == 0:
                origin = lax.rem(z - s + NZ, NZ)
                device, slot = up, s
            else:
                origin = lax.rem(z + s, NZ)
                device, slot = down, nr + s
            src = first_src if s == 0 else at(origin)
            return remote(src, at(origin), ss.at[slot], rs.at[slot], device)

        def step(s):
            for direction, count in ((0, nr), (1, nl)):
                if s >= 1 and s - 1 < count:
                    hop(direction, s - 1).wait_recv()
                if s < count:
                    copy = hop(direction, s)
                    copy.start()
                    waits.append(copy)

        return step, max(nr, nl) + 1

    def gather_item(kind, m, c):
        src = (xin_ref.at[m] if kind == 0 else own_grad.at[m]).at[:, pl.ds(c * W, W)]
        return ring_items(
            src, lambda o: gathered.at[kind, m, c, o], ag_ss.at[kind, m, c], ag_rs.at[kind, m, c], STEPS[c]
        )

    def place_own(kind, m):
        for c in range(HALVES):
            src = xin_ref[m] if kind == 0 else own_grad[m]
            gathered[kind, m, c, z] = src[:, c * W : (c + 1) * W]

    def run_items(items, lag=2):
        order = sorted((i + lag * s, i, s) for i, (_, n) in enumerate(items) for s in range(n))
        for _, i, s in order:
            items[i][0](s)
            if s == items[i][1] - 1 and len(items[i]) > 2:
                pass
            yield i, s == items[i][1] - 1

    def fan_out(buf, dst, ss, rs):
        def send(i, carry):
            peer = plane_peer(i)
            remote(buf.at[peer], dst.at[g], ss, rs, (pipe, peer, z)).start()
            return carry

        lax.fori_loop(1, NG, send, 0)
        dst[g] = buf[g]

    def drained(buf, sem):
        pltpu.make_async_copy(buf.at[pl.ds(0, NG - 1)], buf.at[pl.ds(0, NG - 1)], sem).wait()

    row_e = lax.broadcasted_iota(jnp.int32, (ROWS, EXTRA), 0) // TOK * 4 + z // 2
    row_lane = lax.broadcasted_iota(jnp.int32, (ROWS, EXTRA), 1)

    def build_maps():
        sel_slot = (row_lane == row_e).astype(BF16)
        sel_prob = (row_lane == row_e + 64).astype(BF16)
        r0 = lax.broadcasted_iota(jnp.int32, (ROWS, ALL), 0)
        t1 = lax.broadcasted_iota(jnp.int32, (ROWS, ALL), 1)
        want0 = jnp.where(r0 % TOK // SLOTS == t1 // TOK, r0 % SLOTS + 1, -1).astype(F32)
        r1 = lax.broadcasted_iota(jnp.int32, (ALL, ROWS), 1)
        t0 = lax.broadcasted_iota(jnp.int32, (ALL, ROWS), 0)
        want1 = jnp.where(r1 % TOK // SLOTS == t0 // TOK, r1 % SLOTS + 1, -1).astype(F32)
        for m in range(2):
            table = meta[:, m].reshape(ALL, EXTRA)
            dmat[m] = (nt_dot(sel_slot, table) == want0).astype(BF16)
            hit = nt_dot(table, sel_slot) == want1
            mmat[m] = hit.astype(BF16)
            cmat[m] = jnp.where(hit, nt_dot(table, sel_prob), 0.0).astype(BF16)

    def dispatch(kind, m, c):
        tokens = gathered[kind, m, c].reshape(ALL, W)
        half = ROWS // 2

        def pick(i, carry):
            rows = dmat[m, pl.ds(i * half, half), :]
            got = jnp.dot(rows, tokens, preferred_element_type=F32).astype(BF16)
            picked[kind, m, c, pl.ds(i * NG // 2, NG // 2)] = got.reshape(NG // 2, TOK, W)
            return carry

        lax.fori_loop(0, 2, pick, 0)
        fan_out(picked.at[kind, m, c], arrived.at[kind, m, c], x_ss.at[kind, m, c], x_rs.at[kind, m, c])

    def project(kind, m, c, pairs):
        drained(arrived.at[kind, m, c], x_rs.at[kind, m, c])
        blocks = NG // 2

        def part(i, carry):
            rows = arrived[kind, m, c, pl.ds(i * blocks, blocks)].reshape(blocks * TOK, W)
            at = pl.ds(pl.multiple_of(i * blocks * TOK, blocks * TOK), blocks * TOK)
            for weight, acc in pairs:
                value = nt_dot(rows, weight[:, c * W : (c + 1) * W])
                acc[at, :] = value if c == 0 else acc[at, :] + value
            return carry

        lax.fori_loop(0, 2, part, 0)

    def activate(m):
        step_rows = 64
        e_me = 4 * g + z // 2
        gate_lane = lax.broadcasted_iota(jnp.int32, (step_rows, EXTRA), 1)

        def part(i, carry):
            at = pl.ds(pl.multiple_of(i * step_rows, step_rows), step_rows)
            a, b, q = a_acc[at, :], b_acc[at, :], q_acc[at, :]
            sig = 0.5 * jnp.tanh(0.5 * a) + 0.5
            silu = a * sig
            qs = q * silu
            gate = jnp.sum(qs * b, axis=1, keepdims=True)
            da_buf[at, :] = (q * b * sig * (1.0 + a * (1.0 - sig))).astype(BF16)
            db_buf[at, :] = qs.astype(BF16)
            extra = jnp.where(gate_lane == e_me, gate, 0.0).astype(BF16)
            n = step_rows // TOK
            sent_wide[m, pl.ds(i * n, n), :, W:] = extra.reshape(n, TOK, EXTRA)
            return carry

        lax.fori_loop(0, ROWS // step_rows, part, 0)

    def send_back(m, c):
        blocks = NG // 2

        def part(i, carry):
            at = pl.ds(pl.multiple_of(i * blocks * TOK, blocks * TOK), blocks * TOK)
            cols = slice(c * W, (c + 1) * W)
            u = jnp.dot(da_buf[at, :], wg[:, cols], preferred_element_type=F32)
            u = u + jnp.dot(db_buf[at, :], wu[:, cols], preferred_element_type=F32)
            back_out[c][m, pl.ds(i * blocks, blocks), :, :W] = u.astype(BF16).reshape(blocks, TOK, W)
            return carry

        lax.fori_loop(0, 2, part, 0)
        fan_out(back_out[c].at[m], came_back[c].at[m], r_ss.at[m, c], r_rs.at[m, c])

    def combine(m, c):
        buf = came_back[c]
        drained(buf.at[m], r_rs.at[m, c])
        rows = buf[m].reshape(ROWS, WIDE[c])
        half = ALL // 2

        def part(i, carry):
            at = pl.ds(pl.multiple_of(i * half, half), half)
            n = half // TOK
            value = jnp.dot(cmat[m, at, :], rows[:, :W], preferred_element_type=F32)
            sums[c][pl.ds(i * n, n), :, :W] = value.reshape(n, TOK, W)
            if c == 1:
                extra = jnp.dot(mmat[m, at, :], rows[:, W:], preferred_element_type=F32)
                sums[c][pl.ds(i * n, n), :, W:] = extra.reshape(n, TOK, EXTRA)
            return carry

        lax.fori_loop(0, 2, part, 0)

    def scatter_item(m, c):
        nr, nl = STEPS[c]
        width = WIDE[c]

        def buf(ref, slot):
            return ref.at[m, c, slot, :, pl.ds(0, width)]

        def hop(direction, s):
            slot, device = (s, up) if direction == 0 else (nr + s, down)
            return remote(
                buf(rs_send, slot), buf(rs_recv, slot), rs_ss.at[m, c, slot], rs_rs.at[m, c, slot], device
            )

        def step(s):
            for direction, count in ((0, nr), (1, nl)):
                if s >= 1 and s - 1 < count:
                    hop(direction, s - 1).wait_recv()
                if s < count:
                    slot = s if direction == 0 else nr + s
                    dest = lax.rem(z + nr - s, NZ) if direction == 0 else lax.rem(z - nl + s + NZ, NZ)
                    value = sums[c][dest]
                    if s >= 1:
                        value = value + rs_recv[m, c, slot - 1, :, :width].astype(F32)
                    rs_send[m, c, slot, :, :width] = value.astype(BF16)
                    copy = hop(direction, s)
                    copy.start()
                    waits.append(copy)

        return step, max(nr, nl) + 1

    def finish(m):
        for c in range(HALVES):
            nr, nl = STEPS[c]
            width = WIDE[c]
            total = sums[c][z]
            total += rs_recv[m, c, nr - 1, :, :width].astype(F32)
            total += rs_recv[m, c, nr + nl - 1, :, :width].astype(F32)
            cols = slice(c * W, (c + 1) * W)
            value = (own_grad[m, :, cols].astype(F32) + total[:, :W]).astype(BF16)
            out_ref[m, :, cols] = value
            if m == 0:
                finished[:, cols] = value
            if c == 1:
                extra = total[:, W:]
                ids = ids_ref[m]
                gates = [
                    jnp.sum(jnp.where(lane == ids[:, k : k + 1], extra, 0.0), axis=1, keepdims=True)
                    for k in range(ids.shape[1])
                ]
                gate_ref[m] = jnp.concatenate(gates, axis=1).astype(BF16)

    def run(items):
        order = sorted((i + 2 * s, i, s) for i, (_, n) in enumerate(items) for s in range(n))
        done = []
        for _, i, s in order:
            items[i][0](s)
            if s == items[i][1] - 1:
                done.append(i)
        return done

    place_own(0, 0)
    place_own(1, 0)
    place_own(0, 1)
    meta_item = ring_items(meta.at[z], lambda o: meta.at[o], meta_ss, meta_rs, STEPS[0])
    first = [meta_item] + [gather_item(k, 0, c) for k in range(2) for c in range(HALVES)]
    order = sorted((i + 2 * s, i, s) for i, (_, n) in enumerate(first) for s in range(n))
    for _, i, s in order:
        first[i][0](s)
        if s == first[i][1] - 1:
            if i == 0:
                build_maps()
            else:
                dispatch((i - 1) // HALVES, 0, (i - 1) % HALVES)
    run([gather_item(0, 1, c) for c in range(HALVES)])
    loads[0].wait()
    loads[1].wait()
    for c in range(HALVES):
        project(0, 0, c, ((wg, a_acc), (wu, b_acc)))
    loads[2].wait()
    for c in range(HALVES):
        project(1, 0, c, ((wd, q_acc),))
    activate(0)
    for c in range(HALVES):
        send_back(0, c)
    for c in range(HALVES):
        dispatch(0, 1, c)
    for c in range(HALVES):
        combine(0, c)
    run([scatter_item(0, c) for c in range(HALVES)])
    finish(0)
    hand = remote(finished, passed, pass_ss, pass_rs, partner)
    hand.start()
    hand.wait()
    own_grad[1] = jnp.where(is_last, og_ref[1].astype(F32), passed[...].astype(F32)).astype(BF16)
    place_own(1, 1)
    second = [gather_item(1, 1, c) for c in range(HALVES)]
    order = sorted((i + 2 * s, i, s) for i, (_, n) in enumerate(second) for s in range(n))
    for _, i, s in order:
        second[i][0](s)
        if s == second[i][1] - 1:
            dispatch(1, 1, i)
    for c in range(HALVES):
        project(0, 1, c, ((wg, a_acc), (wu, b_acc)))
    for c in range(HALVES):
        project(1, 1, c, ((wd, q_acc),))
    activate(1)
    for c in range(HALVES):
        send_back(1, c)
    for c in range(HALVES):
        combine(1, c)
    run([scatter_item(1, c) for c in range(HALVES)])
    finish(1)
    for copy in waits:
        copy.wait_send()
    for m in range(2):
        for c in range(HALVES):
            for kind in range(2):
                drained(picked.at[kind, m, c], x_ss.at[kind, m, c])
            drained(back_out[c].at[m], r_ss.at[m, c])


def local(og, cg, xin, ids, prob, gate_weight, up_weight, down_weight):
    vmem = pl.BlockSpec(memory_space=pltpu.VMEM)
    hbm = pl.BlockSpec(memory_space=pl.ANY)
    dma = pltpu.SemaphoreType.DMA
    out, gate = pl.pallas_call(
        kernel,
        out_shape=(
            jax.ShapeDtypeStruct((2, TOK, D), BF16),
            jax.ShapeDtypeStruct((2, TOK, ids.shape[-1]), BF16),
        ),
        in_specs=[vmem] * 5 + [hbm] * 3,
        out_specs=(vmem, vmem),
        scratch_shapes=[
            pltpu.VMEM((HALF, D), BF16),
            pltpu.VMEM((HALF, D), BF16),
            pltpu.VMEM((HALF, D), BF16),
            pltpu.VMEM((NZ, 2, TOK, EXTRA), BF16),
            pltpu.VMEM((2, TOK, D), BF16),
            pltpu.VMEM((TOK, D), BF16),
            pltpu.VMEM((TOK, D), BF16),
            pltpu.VMEM((2, 2, HALVES, NZ, TOK, W), BF16),
            pltpu.VMEM((2, 2, HALVES, NG, TOK, W), BF16),
            pltpu.VMEM((2, 2, HALVES, NG, TOK, W), BF16),
            pltpu.VMEM((2, NG, TOK, WIDE[0]), BF16),
            pltpu.VMEM((2, NG, TOK, WIDE[0]), BF16),
            pltpu.VMEM((2, NG, TOK, WIDE[1]), BF16),
            pltpu.VMEM((2, NG, TOK, WIDE[1]), BF16),
            pltpu.VMEM((ROWS, HALF), F32),
            pltpu.VMEM((ROWS, HALF), F32),
            pltpu.VMEM((ROWS, HALF), F32),
            pltpu.VMEM((ROWS, HALF), BF16),
            pltpu.VMEM((ROWS, HALF), BF16),
            pltpu.VMEM((2, ROWS, ALL), BF16),
            pltpu.VMEM((2, ALL, ROWS), BF16),
            pltpu.VMEM((2, ALL, ROWS), BF16),
            pltpu.VMEM((NZ, TOK, WIDE[0]), F32),
            pltpu.VMEM((NZ, TOK, WIDE[1]), F32),
            pltpu.VMEM((2, HALVES, NZ - 1, TOK, WIDE[1]), BF16),
            pltpu.VMEM((2, HALVES, NZ - 1, TOK, WIDE[1]), BF16),
            dma((3,)),
            dma((NZ - 1,)),
            dma((NZ - 1,)),
            dma((2, 2, HALVES, NZ - 1)),
            dma((2, 2, HALVES, NZ - 1)),
            dma((2, 2, HALVES)),
            dma((2, 2, HALVES)),
            dma((2, HALVES)),
            dma((2, HALVES)),
            dma((2, HALVES, NZ - 1)),
            dma((2, HALVES, NZ - 1)),
            dma,
            dma,
        ],
        compiler_params=pltpu.CompilerParams(
            collective_id=0, has_side_effects=True, vmem_limit_bytes=63 * 2**20
        ),
    )(
        og,
        cg,
        xin[0],
        ids[0],
        prob[0],
        gate_weight[0, 0].T,
        up_weight[0, 0].T,
        down_weight[0, 0],
    )
    return out[None], gate[None]


def solution(mesh):
    rows = ("group", "local")
    return jax.shard_map(
        local,
        mesh=mesh,
        in_specs=(
            P(None, rows, None),
            P(rows, None),
            P("pipe", None, rows, None),
            P("pipe", None, rows, None),
            P("pipe", None, rows, None),
            P("pipe", rows, None, None),
            P("pipe", rows, None, None),
            P("pipe", rows, None, None),
        ),
        out_specs=(P("pipe", None, rows, None), P("pipe", None, rows, None)),
        check_vma=False,
    )
```

```python
import functools

import jax
import jax.numpy as jnp
from jax import lax
from jax.experimental import pallas as pl
from jax.experimental.pallas import tpu as pltpu
from jax.sharding import PartitionSpec as P

MESH = pl.DeviceIdType.MESH
NX, NY, NZ = 4, 4, 8
NG = NX * NY
TOK, D, HALF, SLOTS = 32, 2048, 704, 4
ROWS = NG * TOK
ALL = NZ * TOK
HALVES = 2
W = D // HALVES
EXTRA = 128
WIDE = (W, W + EXTRA)
STEPS = ((4, 3), (3, 4))
NT = (((1,), (1,)), ((), ()))
F32, BF16 = jnp.float32, jnp.bfloat16


def nt_dot(a, b):
    return lax.dot_general(a, b, NT, preferred_element_type=F32)


def kernel(
    og_ref, cg_ref, xin_ref, ids_ref, pr_ref, wg_hbm, wu_hbm, wd_hbm,
    out_ref, gate_ref,
    wg, wu, wd, meta, own_grad, passed, finished,
    gathered, x_picked, x_arrived, g_picked, g_arrived,
    back0, back1, came0, came1,
    a_acc, b_acc, q_acc, da_buf, db_buf, xmat, dmat, cmat, mmat, p0, p1, rs_send, rs_recv,
    w_sem, meta_ss, meta_rs, ag_ss, ag_rs, x_ss, x_rs, f_ss, f_rs, g_ss, g_rs,
    r_ss, r_rs, rs_ss, rs_rs, pass_ss, pass_rs,
):
    pipe = lax.axis_index("pipe")
    g = lax.axis_index("group")
    z = lax.axis_index("local")
    x, y = g // NY, g % NY
    side = z % 2
    base = z - side
    expert = 4 * g + z // 2
    up = (pipe, g, lax.rem(z + 1, NZ))
    down = (pipe, g, lax.rem(z + NZ - 1, NZ))
    mate = (pipe, g, z + 1 - 2 * side)
    partner = (1 - pipe, g, z)
    back, came, sums = (back0, back1), (came0, came1), (p0, p1)
    is_even, is_odd = side == 0, side == 1
    first, last = pipe == 0, pipe == 1
    top = ids_ref.shape[0]
    closing = []

    def remote(src, dst, ss, rs, device):
        return pltpu.make_async_remote_copy(
            src_ref=src, dst_ref=dst, send_sem=ss, recv_sem=rs, device_id=device, device_id_type=MESH
        )

    loads = []
    for i, (h, v) in enumerate(((wg_hbm, wg), (wu_hbm, wu), (wd_hbm, wd))):
        load = pltpu.make_async_copy(h, v, w_sem.at[i])
        load.start()
        loads.append(load)

    barrier = pltpu.get_barrier_semaphore()

    def plane_peer(i):
        dx = i % NX
        dy = lax.rem(i // NX - dx + NY, NY)
        return lax.rem(x + dx, NX) * NY + lax.rem(y + dy, NY)

    def greet(i, carry):
        pl.semaphore_signal(barrier, inc=1, device_id=(pipe, plane_peer(i), z), device_id_type=MESH)
        return carry

    for device in (up, down, partner):
        pl.semaphore_signal(barrier, inc=1, device_id=device, device_id_type=MESH)
    lax.fori_loop(1, NG, greet, 0)

    lane = lax.broadcasted_iota(jnp.int32, (TOK, EXTRA), 1)
    i0 = lax.broadcasted_iota(jnp.int32, (TOK, TOK), 0)
    i1 = lax.broadcasted_iota(jnp.int32, (TOK, TOK), 1)
    lower = (i0 > i1).astype(BF16)
    same = (i0 == i1).astype(BF16)

    def columns(ref, m):
        rows = jnp.concatenate([ref[k, pl.ds(m, 1), :].astype(F32) for k in range(top)], axis=0)
        return nt_dot(same, rows.astype(BF16))

    ids = [columns(ids_ref, m).astype(jnp.int32) for m in range(2)]
    for m in range(2):
        probs = columns(pr_ref, m)
        chosen = jnp.zeros((TOK, EXTRA), F32)
        weight = jnp.zeros((TOK, EXTRA), F32)
        for k in range(top):
            chosen += (lane == ids[m][:, k : k + 1]).astype(F32)
            weight += jnp.where(lane == ids[m][:, k : k + 1] + 64, probs[:, k : k + 1], 0.0)
        before = jnp.dot(lower, chosen.astype(BF16), preferred_element_type=F32)
        meta[z, m] = (chosen * (before + 1.0) + weight).astype(BF16)
    own_grad[0] = jnp.where(last, og_ref[0].astype(F32), cg_ref[...].astype(F32)).astype(BF16)

    def place_own(kind, m):
        src = xin_ref[m] if kind == 0 else own_grad[m]
        for c in range(HALVES):
            gathered[kind, m, c, z] = src[:, c * W : (c + 1) * W]

    place_own(0, 0)
    place_own(1, 0)
    place_own(0, 1)
    pl.semaphore_wait(barrier, NG - 1 + 3)

    def run(items, hooks=None):
        lead = 2 if hooks and len(items) > 2 else 0
        order = sorted(((i if i or not lead else -lead) + 2 * s, i, s) for i, (_, n) in enumerate(items) for s in range(n))
        for _, i, s in order:
            items[i][0](s)
            if hooks and s == items[i][1] - 1:
                hooks[i]()

    def ring(own, at, ss, rs, counts):
        nr, nl = counts

        def hop(direction, s):
            if direction == 0:
                origin, device, slot = lax.rem(z - s + NZ, NZ), up, s
            else:
                origin, device, slot = lax.rem(z + s, NZ), down, nr + s
            return remote(own if s == 0 else at(origin), at(origin), ss.at[slot], rs.at[slot], device)

        def step(s):
            for direction, count in ((0, nr), (1, nl)):
                if s >= 1 and s - 1 < count:
                    hop(direction, s - 1).wait_recv()
                if s < count:
                    hop(direction, s).start()

        for direction, count in ((0, nr), (1, nl)):
            for s in range(count):
                closing.append(lambda d=direction, s=s: hop(d, s).wait_send())
        return step, max(nr, nl) + 1

    def half_ring(own, at, ss, rs):
        def hop(direction, s):
            if direction == 0:
                origin, device, slot = lax.rem(z - s + NZ, NZ), up, s
            else:
                origin, device, slot = lax.rem(z + s, NZ), down, 3 + s
            return remote(own if s == 0 else at(origin), at(origin), ss.at[slot], rs.at[slot], device)

        def step(s):
            for direction in range(2):
                sends, takes = (is_odd, is_even) if direction == 0 else (is_even, is_odd)
                if s in (1, 2):
                    hop(direction, s - 1).wait_recv()
                if s == 3:
                    pl.when(takes)(lambda: hop(direction, 2).wait_recv())
                if s < 2:
                    hop(direction, s).start()
                if s == 2:
                    pl.when(sends)(lambda: hop(direction, 2).start())

        for direction in range(2):
            for s in range(2):
                closing.append(lambda d=direction, s=s: hop(d, s).wait_send())
            sends = is_odd if direction == 0 else is_even
            closing.append(lambda d=direction, k=sends: pl.when(k)(lambda: hop(d, 2).wait_send()))
        return step, 4

    def gather(kind, m, c):
        src = (xin_ref if kind == 0 else own_grad).at[m, :, pl.ds(c * W, W)]
        at = lambda o: gathered.at[kind, m, c, o]
        ss, rs = ag_ss.at[kind, m, c], ag_rs.at[kind, m, c]
        return half_ring(src, at, ss, rs) if kind == 0 else ring(src, at, ss, rs, STEPS[c])

    def fan_out(src, dst, ss, rs):
        def send(i, carry):
            peer = plane_peer(i)
            remote(src(peer), dst(g), ss, rs, (pipe, peer, z)).start()
            return carry

        lax.fori_loop(1, NG, send, 0)

    def drain(ref, sem):
        pltpu.make_async_copy(ref, ref, sem).wait()

    def origin_of(order):
        return lax.rem(base - 3 + NZ + order, NZ)

    def iota(shape, dim):
        return lax.broadcasted_iota(jnp.int32, shape, dim)

    def build_x_maps():
        hr = TOK // 2
        sel = (iota((NG * hr, EXTRA), 1) == iota((NG * hr, EXTRA), 0) // hr * 4 + z // 2).astype(BF16)
        r, t = iota((NG * hr, ALL // 2), 0), iota((NG * hr, ALL // 2), 1)
        want = jnp.where(r % hr // SLOTS == t // TOK, r % SLOTS + 1, -1).astype(F32)
        for m in range(2):
            near = jnp.concatenate([meta[origin_of(4 * side + j), m] for j in range(4)], axis=0)
            xmat[m] = (nt_dot(sel, near) == want).astype(BF16)

    def build_maps():
        e_lane = iota((ROWS, EXTRA), 1)
        e_row = iota((ROWS, EXTRA), 0) // TOK * 4 + z // 2
        sel_slot = (e_lane == e_row).astype(BF16)
        sel_prob = (e_lane == e_row + 64).astype(BF16)
        r, t = iota((ROWS, ALL), 0), iota((ROWS, ALL), 1)
        want0 = jnp.where(origin_of(r % TOK // SLOTS) == t // TOK, r % SLOTS + 1, -1).astype(F32)
        r, t = iota((ALL, ROWS), 1), iota((ALL, ROWS), 0)
        want1 = jnp.where(origin_of(r % TOK // SLOTS) == t // TOK, r % SLOTS + 1, -1).astype(F32)
        for m in range(2):
            table = meta[:, m].reshape(ALL, EXTRA)
            dmat[m] = (nt_dot(sel_slot, table) == want0).astype(BF16)
            hit = nt_dot(table, sel_slot) == want1
            mmat[m] = hit.astype(BF16)
            cmat[m] = jnp.where(hit, nt_dot(table, sel_prob), 0.0).astype(BF16)

    my_half = pl.ds(pl.multiple_of(side * (TOK // 2), TOK // 2), TOK // 2)

    def dispatch_x(m, c):
        tokens = jnp.concatenate([gathered[0, m, c, origin_of(4 * side + j)] for j in range(4)], axis=0)
        rows = jnp.dot(xmat[m], tokens, preferred_element_type=F32).astype(BF16)
        x_picked[m, c] = rows.reshape(NG, TOK // 2, W)
        fan_out(
            lambda peer: x_picked.at[m, c, peer],
            lambda col: x_arrived.at[m, c, col, my_half, :],
            x_ss.at[m, c],
            x_rs.at[m, c],
        )
        x_arrived[m, c, g, my_half, :] = x_picked[m, c, g]

    def forward(m, c):
        block = x_arrived.at[m, c, :, my_half, :]
        return remote(block, block, f_ss.at[m, c], f_rs.at[m, c], mate)

    def forward_x(m, c):
        drain(x_picked.at[m, c, pl.ds(0, NG - 1)], x_rs.at[m, c])
        forward(m, c).start()

    def dispatch_g(m, c):
        tokens = gathered[1, m, c].reshape(ALL, W)
        rows = jnp.dot(dmat[m], tokens, preferred_element_type=F32).astype(BF16)
        g_picked[m, c] = rows.reshape(NG, TOK, W)
        fan_out(
            lambda peer: g_picked.at[m, c, peer],
            lambda col: g_arrived.at[m, c, col],
            g_ss.at[m, c],
            g_rs.at[m, c],
        )
        g_arrived[m, c, g] = g_picked[m, c, g]

    def project(rows_ref, c, pairs):
        rows = rows_ref[...].reshape(ROWS, W)
        for weight, acc in pairs:
            value = nt_dot(rows, weight[:, c * W : (c + 1) * W])
            acc[...] = value if c == 0 else acc[...] + value

    def project_x(m, c):
        forward(m, c).wait_recv()
        project(x_arrived.at[m, c], c, ((wg, a_acc), (wu, b_acc)))

    def project_g(m, c):
        drain(g_arrived.at[m, c, pl.ds(0, NG - 1)], g_rs.at[m, c])
        project(g_arrived.at[m, c], c, ((wd, q_acc),))

    def activate(m):
        step_rows = 128
        gate_lane = iota((step_rows, EXTRA), 1)

        def part(i, carry):
            at = pl.ds(pl.multiple_of(i * step_rows, step_rows), step_rows)
            a, b, q = a_acc[at, :], b_acc[at, :], q_acc[at, :]
            sig = 0.5 * jnp.tanh(0.5 * a) + 0.5
            silu = a * sig
            qs = q * silu
            gate = jnp.sum(qs * b, axis=1, keepdims=True)
            da_buf[at, :] = (q * b * sig * (1.0 + a * (1.0 - sig))).astype(BF16)
            db_buf[at, :] = qs.astype(BF16)
            extra = jnp.where(gate_lane == expert, gate, 0.0).astype(BF16)
            n = step_rows // TOK
            back1[m, pl.ds(i * n, n), :, W:] = extra.reshape(n, TOK, EXTRA)
            return carry

        lax.fori_loop(0, ROWS // step_rows, part, 0)

    def send_back(m, c):
        cols = slice(c * W, (c + 1) * W)
        u = jnp.dot(da_buf[...], wg[:, cols], preferred_element_type=F32)
        u = u + jnp.dot(db_buf[...], wu[:, cols], preferred_element_type=F32)
        back[c][m, :, :, :W] = u.astype(BF16).reshape(NG, TOK, W)
        fan_out(
            lambda peer: back[c].at[m, peer], lambda col: came[c].at[m, col], r_ss.at[m, c], r_rs.at[m, c]
        )
        came[c][m, g] = back[c][m, g]

    def combine(m, c):
        drain(came[c].at[m, pl.ds(0, NG - 1)], r_rs.at[m, c])
        rows = came[c][m].reshape(ROWS, WIDE[c])
        value = jnp.dot(cmat[m], rows[:, :W], preferred_element_type=F32)
        sums[c][:, :, :W] = value.reshape(NZ, TOK, W)
        if c == 1:
            extra = jnp.dot(mmat[m], rows[:, W:], preferred_element_type=F32)
            sums[c][:, :, W:] = extra.reshape(NZ, TOK, EXTRA)

    def scatter(m, c):
        nr, nl = STEPS[c]
        width = WIDE[c]

        def buf(ref, slot):
            return ref.at[m, c, slot, :, pl.ds(0, width)]

        def hop(direction, s):
            slot, device = (s, up) if direction == 0 else (nr + s, down)
            return remote(
                buf(rs_send, slot), buf(rs_recv, slot), rs_ss.at[m, c, slot], rs_rs.at[m, c, slot], device
            )

        def step(s):
            for direction, count in ((0, nr), (1, nl)):
                if s >= 1 and s - 1 < count:
                    hop(direction, s - 1).wait_recv()
                if s < count:
                    slot = s if direction == 0 else nr + s
                    dest = lax.rem(z + nr - s, NZ) if direction == 0 else lax.rem(z - nl + s + NZ, NZ)
                    value = sums[c][dest]
                    if s >= 1:
                        value = value + rs_recv[m, c, slot - 1, :, :width].astype(F32)
                    rs_send[m, c, slot, :, :width] = value.astype(BF16)
                    hop(direction, s).start()

        def close():
            for direction, count in ((0, nr), (1, nl)):
                for s in range(count):
                    hop(direction, s).wait_send()

        return (step, max(nr, nl) + 1), close

    def finish(m):
        for c in range(HALVES):
            nr, nl = STEPS[c]
            width = WIDE[c]
            total = sums[c][z]
            total += rs_recv[m, c, nr - 1, :, :width].astype(F32)
            total += rs_recv[m, c, nr + nl - 1, :, :width].astype(F32)
            cols = slice(c * W, (c + 1) * W)
            value = (own_grad[m, :, cols].astype(F32) + total[:, :W]).astype(BF16)
            out_ref[m, :, cols] = value
            if m == 0:
                finished[:, cols] = value
            if c == 1:
                extra = total[:, W:]
                gates = jnp.zeros((TOK, EXTRA), F32)
                for k in range(top):
                    picked = jnp.sum(jnp.where(lane == ids[m][:, k : k + 1], extra, 0.0), axis=1, keepdims=True)
                    gates += jnp.where(lane == k, picked, 0.0)
                flat = lax.dot_general(
                    gates.astype(BF16), same, (((0,), (0,)), ((), ())), preferred_element_type=F32
                ).astype(BF16)
                for k in range(top):
                    gate_ref[k, pl.ds(m, 1), :] = flat[k : k + 1, :]

    def collect(m):
        for c in range(HALVES):
            combine(m, c)
        run([scatter(m, c)[0] for c in range(HALVES)])
        finish(m)

    both = range(HALVES)
    handed = lambda: remote(finished, passed, pass_ss, pass_rs, partner)
    late = [gather(1, 1, c) for c in both]

    def late_gradients():
        place_own(1, 1)
        run(late, [lambda c=c: dispatch_g(1, c) for c in both])

    def early_part(c):
        dispatch_g(0, c)
        forward_x(0, c)

    items = [ring(meta.at[z], lambda o: meta.at[o], meta_ss, meta_rs, STEPS[0])]
    items += [gather(0, 0, c) for c in both] + [gather(1, 0, c) for c in both] + [gather(0, 1, c) for c in both]
    def second_x():
        dispatch_x(0, 1)
        build_maps()

    hooks = [build_x_maps, lambda: dispatch_x(0, 0), second_x]
    hooks += [lambda c=c: early_part(c) for c in both]
    hooks += [lambda: None] * 2
    run(items, hooks)

    @pl.when(first)
    def _():
        for c in both:
            dispatch_x(1, c)

    loads[0].wait()
    loads[1].wait()
    for c in both:
        project_x(0, c)
    loads[2].wait()
    for c in both:
        project_g(0, c)
    activate(0)
    for c in both:
        send_back(0, c)

    @pl.when(last)
    def _():
        own_grad[1] = og_ref[1]
        for c in both:
            dispatch_x(1, c)
        late_gradients()
        collect(0)
        handed().start()
        for c in both:
            forward_x(1, c)
        handed().wait_send()

    @pl.when(first)
    def _():
        for c in both:
            forward_x(1, c)
        handed().wait_recv()
        own_grad[1] = passed[...]
        late_gradients()
        collect(0)

    for c in both:
        project_x(1, c)
    for c in both:
        project_g(1, c)
    activate(1)
    for c in both:
        send_back(1, c)
    collect(1)

    for close in closing:
        close()
    for m in range(2):
        for c in both:
            scatter(m, c)[1]()
            forward(m, c).wait_send()
            drain(x_picked.at[m, c, pl.ds(0, NG - 1)], x_ss.at[m, c])
            drain(g_picked.at[m, c, pl.ds(0, NG - 1)], g_ss.at[m, c])
            drain(back[c].at[m, pl.ds(0, NG - 1)], r_ss.at[m, c])


def local(og, cg, xin, ids, prob, gate_weight, up_weight, down_weight):
    vmem = pl.BlockSpec(memory_space=pltpu.VMEM)
    hbm = pl.BlockSpec(memory_space=pl.ANY)
    dma = pltpu.SemaphoreType.DMA
    top = ids.shape[-1]
    both = (2, HALVES)
    hops = (NZ - 1,)
    out, gate = pl.pallas_call(
        kernel,
        out_shape=(
            jax.ShapeDtypeStruct((2, TOK, D), BF16),
            jax.ShapeDtypeStruct((top, 2, TOK), BF16),
        ),
        in_specs=[vmem] * 5 + [hbm] * 3,
        out_specs=(vmem, vmem),
        scratch_shapes=[
            pltpu.VMEM((HALF, D), BF16),
            pltpu.VMEM((HALF, D), BF16),
            pltpu.VMEM((HALF, D), BF16),
            pltpu.VMEM((NZ, 2, TOK, EXTRA), BF16),
            pltpu.VMEM((2, TOK, D), BF16),
            pltpu.VMEM((TOK, D), BF16),
            pltpu.VMEM((TOK, D), BF16),
            pltpu.VMEM((2, *both, NZ, TOK, W), BF16),
            pltpu.VMEM((*both, NG, TOK // 2, W), BF16),
            pltpu.VMEM((*both, NG, TOK, W), BF16),
            pltpu.VMEM((*both, NG, TOK, W), BF16),
            pltpu.VMEM((*both, NG, TOK, W), BF16),
            pltpu.VMEM((2, NG, TOK, WIDE[0]), BF16),
            pltpu.VMEM((2, NG, TOK, WIDE[1]), BF16),
            pltpu.VMEM((2, NG, TOK, WIDE[0]), BF16),
            pltpu.VMEM((2, NG, TOK, WIDE[1]), BF16),
            pltpu.VMEM((ROWS, HALF), F32),
            pltpu.VMEM((ROWS, HALF), F32),
            pltpu.VMEM((ROWS, HALF), F32),
            pltpu.VMEM((ROWS, HALF), BF16),
            pltpu.VMEM((ROWS, HALF), BF16),
            pltpu.VMEM((2, ROWS // 2, ALL // 2), BF16),
            pltpu.VMEM((2, ROWS, ALL), BF16),
            pltpu.VMEM((2, ALL, ROWS), BF16),
            pltpu.VMEM((2, ALL, ROWS), BF16),
            pltpu.VMEM((NZ, TOK, WIDE[0]), F32),
            pltpu.VMEM((NZ, TOK, WIDE[1]), F32),
            pltpu.VMEM((*both, NZ - 1, TOK, WIDE[1]), BF16),
            pltpu.VMEM((*both, NZ - 1, TOK, WIDE[1]), BF16),
            dma((3,)),
            dma(hops),
            dma(hops),
            dma((2, *both, *hops)),
            dma((2, *both, *hops)),
        ]
        + [dma(both)] * 8
        + [dma((*both, *hops))] * 2
        + [dma] * 2,
        compiler_params=pltpu.CompilerParams(
            collective_id=0, has_side_effects=True, vmem_limit_bytes=63 * 2**20
        ),
    )(
        og,
        cg,
        xin[0],
        jnp.transpose(ids[0], (2, 0, 1)),
        jnp.transpose(prob[0], (2, 0, 1)),
        gate_weight[0, 0].T,
        up_weight[0, 0].T,
        down_weight[0, 0],
    )
    return out[None], jnp.transpose(gate, (1, 2, 0))[None]


def solution(mesh):
    rows = ("group", "local")
    return jax.shard_map(
        local,
        mesh=mesh,
        in_specs=(
            P(None, rows, None),
            P(rows, None),
            P("pipe", None, rows, None),
            P("pipe", None, rows, None),
            P("pipe", None, rows, None),
            P("pipe", rows, None, None),
            P("pipe", rows, None, None),
            P("pipe", rows, None, None),
        ),
        out_specs=(P("pipe", None, rows, None), P("pipe", None, rows, None)),
        check_vma=False,
    )
```

```python
import functools

import jax
import jax.numpy as jnp
from jax import lax
from jax.experimental import pallas as pl
from jax.experimental.pallas import tpu as pltpu
from jax.sharding import PartitionSpec as P

MESH = pl.DeviceIdType.MESH
NX, NY, NZ = 4, 4, 8
NG = NX * NY
TOK, D, HALF, SLOTS = 32, 2048, 704, 4
ROWS = NG * TOK
ALL = NZ * TOK
HALVES = 2
W = D // HALVES
EXTRA = 128
WIDE = (W, W + EXTRA)
STEPS = ((4, 3), (3, 4))
NT = (((1,), (1,)), ((), ()))
F32, BF16 = jnp.float32, jnp.bfloat16


def nt_dot(a, b):
    return lax.dot_general(a, b, NT, preferred_element_type=F32)


def kernel(
    og_ref, cg_ref, xin_ref, ids_ref, pr_ref, wg_hbm, wu_hbm, wd_hbm,
    out_ref, gate_ref,
    wg, wu, wd, meta, own_grad, passed, finished,
    gathered, x_picked, x_arrived, g_picked, g_arrived,
    back0, back1, came0, came1,
    a_acc, b_acc, q_acc, da_buf, db_buf, xmat, dmat, cmat, mmat, p0, p1, rs_send, rs_recv,
    w_sem, meta_ss, meta_rs, ag_ss, ag_rs, x_ss, x_rs, f_ss, f_rs, g_ss, g_rs,
    r_ss, r_rs, rs_ss, rs_rs, pass_ss, pass_rs, turn,
):
    pipe = lax.axis_index("pipe")
    g = lax.axis_index("group")
    z = lax.axis_index("local")
    x, y = g // NY, g % NY
    side = z % 2
    base = z - side
    expert = 4 * g + z // 2
    up = (pipe, g, lax.rem(z + 1, NZ))
    down = (pipe, g, lax.rem(z + NZ - 1, NZ))
    mate = (pipe, g, z + 1 - 2 * side)
    partner = (1 - pipe, g, z)
    back, came, sums = (back0, back1), (came0, came1), (p0, p1)
    is_even, is_odd = side == 0, side == 1
    first, last = pipe == 0, pipe == 1
    top = ids_ref.shape[0]

    def remote(src, dst, ss, rs, device):
        return pltpu.make_async_remote_copy(
            src_ref=src, dst_ref=dst, send_sem=ss, recv_sem=rs, device_id=device, device_id_type=MESH
        )

    loads = []
    for i, (h, v) in enumerate(((wg_hbm, wg), (wu_hbm, wu), (wd_hbm, wd))):
        load = pltpu.make_async_copy(h, v, w_sem.at[i])
        loads.append(load)

    barrier = pltpu.get_barrier_semaphore()

    def plane_peer(i):
        dx = i % NX
        dy = lax.rem(i // NX - dx + NY, NY)
        return lax.rem(x + dx, NX) * NY + lax.rem(y + dy, NY)

    def greet(i, carry):
        pl.semaphore_signal(barrier, inc=1, device_id=(pipe, plane_peer(i), z), device_id_type=MESH)
        return carry

    for device in (up, down, partner):
        pl.semaphore_signal(barrier, inc=1, device_id=device, device_id_type=MESH)
    lax.fori_loop(1, NG, greet, 0)

    lane = lax.broadcasted_iota(jnp.int32, (TOK, EXTRA), 1)
    i0 = lax.broadcasted_iota(jnp.int32, (TOK, TOK), 0)
    i1 = lax.broadcasted_iota(jnp.int32, (TOK, TOK), 1)
    lower = (i0 > i1).astype(BF16)
    same = (i0 == i1).astype(BF16)

    def columns(ref, m):
        rows = jnp.concatenate([ref[k, pl.ds(m, 1), :].astype(F32) for k in range(top)], axis=0)
        return nt_dot(same, rows.astype(BF16))

    ids = [columns(ids_ref, m).astype(jnp.int32) for m in range(2)]
    for m in range(2):
        probs = columns(pr_ref, m)
        chosen = jnp.zeros((TOK, EXTRA), F32)
        weight = jnp.zeros((TOK, EXTRA), F32)
        for k in range(top):
            chosen += (lane == ids[m][:, k : k + 1]).astype(F32)
            weight += jnp.where(lane == ids[m][:, k : k + 1] + 64, probs[:, k : k + 1], 0.0)
        before = jnp.dot(lower, chosen.astype(BF16), preferred_element_type=F32)
        meta[z, m] = (chosen * (before + 1.0) + weight).astype(BF16)
    own_grad[0] = jnp.where(last, og_ref[0].astype(F32), cg_ref[...].astype(F32)).astype(BF16)

    def place_own(kind, m):
        src = xin_ref[m] if kind == 0 else own_grad[m]
        for c in range(HALVES):
            gathered[kind, m, c, z] = src[:, c * W : (c + 1) * W]

    place_own(0, 0)
    place_own(1, 0)
    place_own(0, 1)
    pl.semaphore_wait(barrier, NG - 1 + 3)

    def run(items, hooks=None, ahead=0, keys=(0, 1, 2, 3), pace=(2,) * 5):
        order = sorted(
            (keys[i] + pace[i] * s if s or i >= ahead else i - NZ, i, s)
            for i, (_, n, _) in enumerate(items)
            for s in range(n)
        )
        for _, i, s in order:
            items[i][0](s)
            if hooks and s == items[i][1] - 1:
                hooks[i]()

    def ring(own, at, ss, rs, counts):
        nr, nl = counts

        def hop(direction, s):
            if direction == 0:
                origin, device, slot = lax.rem(z - s + NZ, NZ), up, s
            else:
                origin, device, slot = lax.rem(z + s, NZ), down, nr + s
            return remote(own if s == 0 else at(origin), at(origin), ss.at[slot], rs.at[slot], device)

        def step(s):
            for direction, count in ((0, nr), (1, nl)):
                if s >= 1 and s - 1 < count:
                    hop(direction, s - 1).wait_recv()
                if s < count:
                    hop(direction, s).start()

        def close():
            for direction, count in ((0, nr), (1, nl)):
                for s in range(count):
                    hop(direction, s).wait_send()

        return step, max(nr, nl) + 1, close

    def half_ring(own, at, ss, rs):
        def hop(direction, s):
            if direction == 0:
                origin, device, slot = lax.rem(z - s + NZ, NZ), up, s
            else:
                origin, device, slot = lax.rem(z + s, NZ), down, 3 + s
            return remote(own if s == 0 else at(origin), at(origin), ss.at[slot], rs.at[slot], device)

        def step(s):
            for direction in range(2):
                sends, takes = (is_odd, is_even) if direction == 0 else (is_even, is_odd)
                if s in (1, 2):
                    hop(direction, s - 1).wait_recv()
                if s == 3:
                    pl.when(takes)(lambda: hop(direction, 2).wait_recv())
                if s < 2:
                    hop(direction, s).start()
                if s == 2:
                    pl.when(sends)(lambda: hop(direction, 2).start())

        def close():
            for direction in range(2):
                for s in range(2):
                    hop(direction, s).wait_send()
                pl.when(is_odd if direction == 0 else is_even)(lambda: hop(direction, 2).wait_send())

        return step, 4, close

    def gather(kind, m, c, whole):
        src = (xin_ref if kind == 0 else own_grad).at[m, :, pl.ds(c * W, W)]
        at = lambda o: gathered.at[kind, m, c, o]
        ss, rs = ag_ss.at[kind, m, c], ag_rs.at[kind, m, c]
        return ring(src, at, ss, rs, STEPS[c]) if whole else half_ring(src, at, ss, rs)

    def fan_out(src, dst, ss, rs):
        def send(i, carry):
            peer = plane_peer(i)
            remote(src(peer), dst(g), ss, rs, (pipe, peer, z)).start()
            return carry

        lax.fori_loop(1, NG, send, 0)

    def drain(ref, sem):
        pltpu.make_async_copy(ref, ref, sem).wait()

    def origin_of(order):
        return lax.rem(base - 3 + NZ + order, NZ)

    def iota(shape, dim):
        return lax.broadcasted_iota(jnp.int32, shape, dim)

    def build_x_maps():
        hr = TOK // 2
        sel = (iota((NG * hr, EXTRA), 1) == iota((NG * hr, EXTRA), 0) // hr * 4 + z // 2).astype(BF16)
        r, t = iota((NG * hr, ALL // 2), 0), iota((NG * hr, ALL // 2), 1)
        want = jnp.where(r % hr // SLOTS == t // TOK, r % SLOTS + 1, -1).astype(F32)
        for m in range(2):
            near = jnp.concatenate([meta[origin_of(4 * side + j), m] for j in range(4)], axis=0)
            xmat[m] = (nt_dot(sel, near) == want).astype(BF16)

    def build_maps():
        e_lane = iota((ROWS, EXTRA), 1)
        e_row = iota((ROWS, EXTRA), 0) // TOK * 4 + z // 2
        sel_slot = (e_lane == e_row).astype(BF16)
        sel_prob = (e_lane == e_row + 64).astype(BF16)
        r, t = iota((ROWS, ALL), 0), iota((ROWS, ALL), 1)
        want0 = jnp.where(origin_of(r % TOK // SLOTS) == t // TOK, r % SLOTS + 1, -1).astype(F32)
        r, t = iota((ALL, ROWS), 1), iota((ALL, ROWS), 0)
        want1 = jnp.where(origin_of(r % TOK // SLOTS) == t // TOK, r % SLOTS + 1, -1).astype(F32)
        for m in range(2):
            table = meta[:, m].reshape(ALL, EXTRA)
            dmat[m] = (nt_dot(sel_slot, table) == want0).astype(BF16)
            hit = nt_dot(table, sel_slot) == want1
            mmat[m] = hit.astype(BF16)
            cmat[m] = jnp.where(hit, nt_dot(table, sel_prob), 0.0).astype(BF16)

    my_half = pl.ds(pl.multiple_of(side * (TOK // 2), TOK // 2), TOK // 2)

    route = ((x_picked, x_arrived, x_ss, x_rs), (g_picked, g_arrived, g_ss, g_rs))

    def dispatch(kind, m, c):
        picked, arrived, ss, rs = route[kind]
        tokens = gathered[kind, m, c].reshape(ALL, W)
        rows = jnp.dot(dmat[m], tokens, preferred_element_type=F32).astype(BF16)
        picked[m, c] = rows.reshape(NG, TOK, W)
        fan_out(
            lambda peer: picked.at[m, c, peer], lambda col: arrived.at[m, c, col], ss.at[m, c], rs.at[m, c]
        )
        arrived[m, c, g] = picked[m, c, g]

    def dispatch_half(kind, m, c):
        picked, arrived, ss, rs = route[kind]
        tokens = jnp.concatenate([gathered[kind, m, c, origin_of(4 * side + j)] for j in range(4)], axis=0)
        rows = jnp.dot(xmat[m], tokens, preferred_element_type=F32).astype(BF16)
        picked[m, c, :, : TOK // 2, :] = rows.reshape(NG, TOK // 2, W)
        fan_out(
            lambda peer: picked.at[m, c, peer, pl.ds(0, TOK // 2), :],
            lambda col: arrived.at[m, c, col, my_half, :],
            ss.at[m, c],
            rs.at[m, c],
        )
        arrived[m, c, g, my_half, :] = picked[m, c, g, : TOK // 2, :]

    def halves(kind, m, c):
        return route[kind][0].at[m, c, pl.ds(0, NG - 1), pl.ds(0, TOK // 2), :]

    def exchange(kind, m, c, at, count):
        block = route[kind][1].at[m, c, pl.ds(at, count), my_half, :]
        return remote(block, block, f_ss.at[kind, m, c], f_rs.at[kind, m, c], mate)

    def forward(kind, m, c):
        drain(halves(kind, m, c), route[kind][3].at[m, c])
        for part in range(4):
            exchange(kind, m, c, part * NG // 4, NG // 4).start()

    def project(rows_ref, c, pairs):
        rows = rows_ref[...].reshape(ROWS, W)
        for weight, acc in pairs:
            value = nt_dot(rows, weight[:, c * W : (c + 1) * W])
            acc[...] = value if c == 0 else acc[...] + value

    def project_x(m, c):
        exchange(0, m, c, 0, NG).wait_recv()
        project(x_arrived.at[m, c], c, ((wg, a_acc), (wu, b_acc)))

    def project_g(m, c, whole):
        if whole:
            drain(g_arrived.at[m, c, pl.ds(0, NG - 1)], g_rs.at[m, c])
        else:
            exchange(1, m, c, 0, NG).wait_recv()
        project(g_arrived.at[m, c], c, ((wd, q_acc),))

    def activate(m):
        step_rows = 128
        gate_lane = iota((step_rows, EXTRA), 1)

        def part(i, carry):
            at = pl.ds(pl.multiple_of(i * step_rows, step_rows), step_rows)
            a, b, q = a_acc[at, :], b_acc[at, :], q_acc[at, :]
            sig = 0.5 * jnp.tanh(0.5 * a) + 0.5
            silu = a * sig
            qs = q * silu
            gate = jnp.sum(qs * b, axis=1, keepdims=True)
            da_buf[at, :] = (q * b * sig * (1.0 + a * (1.0 - sig))).astype(BF16)
            db_buf[at, :] = qs.astype(BF16)
            extra = jnp.where(gate_lane == expert, gate, 0.0).astype(BF16)
            n = step_rows // TOK
            back1[m, pl.ds(i * n, n), :, W:] = extra.reshape(n, TOK, EXTRA)
            return carry

        lax.fori_loop(0, ROWS // step_rows, part, 0)

    def backward(m, c):
        cols = slice(c * W, (c + 1) * W)
        u = jnp.dot(da_buf[...], wg[:, cols], preferred_element_type=F32)
        u = u + jnp.dot(db_buf[...], wu[:, cols], preferred_element_type=F32)
        back[c][m, :, :, :W] = u.astype(BF16).reshape(NG, TOK, W)

    def send_back(m, c):
        fan_out(
            lambda peer: back[c].at[m, peer], lambda col: came[c].at[m, col], r_ss.at[m, c], r_rs.at[m, c]
        )
        came[c][m, g] = back[c][m, g]

    def combine(m, c):
        drain(came[c].at[m, pl.ds(0, NG - 1)], r_rs.at[m, c])
        rows = came[c][m].reshape(ROWS, WIDE[c])
        value = jnp.dot(cmat[m], rows[:, :W], preferred_element_type=F32)
        sums[c][:, :, :W] = value.reshape(NZ, TOK, W)
        if c == 1:
            extra = jnp.dot(mmat[m], rows[:, W:], preferred_element_type=F32)
            sums[c][:, :, W:] = extra.reshape(NZ, TOK, EXTRA)

    def scatter(m, c):
        nr, nl = STEPS[c]
        width = WIDE[c]

        def buf(ref, slot):
            return ref.at[m, c, slot, :, pl.ds(0, width)]

        def hop(direction, s):
            slot, device = (s, up) if direction == 0 else (nr + s, down)
            return remote(
                buf(rs_send, slot), buf(rs_recv, slot), rs_ss.at[m, c, slot], rs_rs.at[m, c, slot], device
            )

        def step(s):
            for direction, count in ((0, nr), (1, nl)):
                if s >= 1 and s - 1 < count:
                    hop(direction, s - 1).wait_recv()
                if s < count:
                    slot = s if direction == 0 else nr + s
                    dest = lax.rem(z + nr - s, NZ) if direction == 0 else lax.rem(z - nl + s + NZ, NZ)
                    value = sums[c][dest]
                    if s >= 1:
                        value = value + rs_recv[m, c, slot - 1, :, :width].astype(F32)
                    rs_send[m, c, slot, :, :width] = value.astype(BF16)
                    hop(direction, s).start()

        def close():
            for direction, count in ((0, nr), (1, nl)):
                for s in range(count):
                    hop(direction, s).wait_send()

        return step, max(nr, nl) + 1, close

    def finish(m):
        for c in range(HALVES):
            nr, nl = STEPS[c]
            width = WIDE[c]
            total = sums[c][z]
            total += rs_recv[m, c, nr - 1, :, :width].astype(F32)
            total += rs_recv[m, c, nr + nl - 1, :, :width].astype(F32)
            cols = slice(c * W, (c + 1) * W)
            value = (own_grad[m, :, cols].astype(F32) + total[:, :W]).astype(BF16)
            out_ref[m, :, cols] = value
            if m == 0:
                finished[:, cols] = value
            if c == 1:
                extra = total[:, W:]
                gates = jnp.zeros((TOK, EXTRA), F32)
                for k in range(top):
                    picked = jnp.sum(jnp.where(lane == ids[m][:, k : k + 1], extra, 0.0), axis=1, keepdims=True)
                    gates += jnp.where(lane == k, picked, 0.0)
                flat = lax.dot_general(
                    gates.astype(BF16), same, (((0,), (0,)), ((), ())), preferred_element_type=F32
                ).astype(BF16)
                for k in range(top):
                    gate_ref[k, pl.ds(m, 1), :] = flat[k : k + 1, :]

    def collect(m, between=lambda: None):
        for c in range(HALVES):
            combine(m, c)
        between()
        run([scatter(m, c) for c in range(HALVES)])
        finish(m)

    both = range(HALVES)
    handed = lambda: remote(finished, passed, pass_ss, pass_rs, partner)
    second_x = [gather(0, 1, c, False) for c in both]
    half_g = [gather(1, 1, c, False) for c in both]
    whole_g = [gather(1, 1, c, True) for c in both]
    send_x = [lambda c=c: dispatch_half(0, 1, c) for c in both]
    send_half_g = [lambda c=c: dispatch_half(1, 1, c) for c in both]
    send_whole_g = [lambda c=c: dispatch(1, 1, c) for c in both]

    def release():
        pl.semaphore_signal(turn, inc=1, device_id=partner, device_id_type=MESH)

    items = [ring(meta.at[z], lambda o: meta.at[o], meta_ss, meta_rs, STEPS[0])]
    items += [gather(kind, 0, c, kind == 1) for kind in range(2) for c in both]

    def rest_of_x():
        dispatch_half(0, 0, 1)
        build_maps()

    hooks = [build_x_maps, lambda: dispatch_half(0, 0, 0), rest_of_x]
    hooks += [lambda c=c: dispatch(1, 0, c) for c in both]
    run(items, hooks, 3, (-1, 0, 0.5, 3, 4), (1.4, 2, 2, 2, 2))

    for load in loads:
        load.start()

    @pl.when(first)
    def _():
        run(second_x, send_x)

    for c in both:
        forward(0, 0, c)
    for load in loads:
        load.wait()
    for c in both:
        project_x(0, c)
    for c in both:
        project_g(0, c, True)

    @pl.when(first)
    def _():
        for c in both:
            forward(0, 1, c)

    activate(0)
    for c in both:
        backward(0, c)
        pl.when(last)(lambda: send_back(0, c))

    @pl.when(last)
    def _():
        own_grad[1] = og_ref[1]
        place_own(1, 1)
        run(second_x + whole_g, send_x + send_whole_g)
        collect(0, release)
        handed().start()
        for c in both:
            forward(0, 1, c)
        for c in both:
            project_g(1, c, True)
        for c in both:
            project_x(1, c)
        handed().wait_send()

    @pl.when(first)
    def _():
        pl.semaphore_wait(turn, 1)
        for c in both:
            send_back(0, c)
        handed().wait_recv()
        own_grad[1] = passed[...]
        place_own(1, 1)
        run(half_g, send_half_g)
        for c in both:
            forward(1, 1, c)
        for c in both:
            project_x(1, c)
        for c in both:
            project_g(1, c, False)

    activate(1)
    for c in both:
        backward(1, c)
        send_back(1, c)

    @pl.when(first)
    def _():
        collect(0)

    collect(1)

    for item in items + second_x + [scatter(m, c) for m in range(2) for c in both]:
        item[2]()
    for c in both:
        for m in range(2):
            exchange(0, m, c, 0, NG).wait_send()
            drain(halves(0, m, c), x_ss.at[m, c])
            drain(back[c].at[m, pl.ds(0, NG - 1)], r_ss.at[m, c])
        drain(g_picked.at[0, c, pl.ds(0, NG - 1)], g_ss.at[0, c])

    @pl.when(first)
    def _():
        for c in both:
            half_g[c][2]()
            exchange(1, 1, c, 0, NG).wait_send()
            drain(halves(1, 1, c), g_ss.at[1, c])

    @pl.when(last)
    def _():
        for c in both:
            whole_g[c][2]()
            drain(g_picked.at[1, c, pl.ds(0, NG - 1)], g_ss.at[1, c])


def local(og, cg, xin, ids, prob, gate_weight, up_weight, down_weight):
    vmem = pl.BlockSpec(memory_space=pltpu.VMEM)
    hbm = pl.BlockSpec(memory_space=pl.ANY)
    dma = pltpu.SemaphoreType.DMA
    top = ids.shape[-1]
    both = (2, HALVES)
    hops = (NZ - 1,)
    out, gate = pl.pallas_call(
        kernel,
        out_shape=(
            jax.ShapeDtypeStruct((2, TOK, D), BF16),
            jax.ShapeDtypeStruct((top, 2, TOK), BF16),
        ),
        in_specs=[vmem] * 5 + [hbm] * 3,
        out_specs=(vmem, vmem),
        scratch_shapes=[
            pltpu.VMEM((HALF, D), BF16),
            pltpu.VMEM((HALF, D), BF16),
            pltpu.VMEM((HALF, D), BF16),
            pltpu.VMEM((NZ, 2, TOK, EXTRA), BF16),
            pltpu.VMEM((2, TOK, D), BF16),
            pltpu.VMEM((TOK, D), BF16),
            pltpu.VMEM((TOK, D), BF16),
            pltpu.VMEM((2, *both, NZ, TOK, W), BF16),
            pltpu.VMEM((*both, NG, TOK, W), BF16),
            pltpu.VMEM((*both, NG, TOK, W), BF16),
            pltpu.VMEM((*both, NG, TOK, W), BF16),
            pltpu.VMEM((*both, NG, TOK, W), BF16),
            pltpu.VMEM((2, NG, TOK, WIDE[0]), BF16),
            pltpu.VMEM((2, NG, TOK, WIDE[1]), BF16),
            pltpu.VMEM((2, NG, TOK, WIDE[0]), BF16),
            pltpu.VMEM((2, NG, TOK, WIDE[1]), BF16),
            pltpu.VMEM((ROWS, HALF), F32),
            pltpu.VMEM((ROWS, HALF), F32),
            pltpu.VMEM((ROWS, HALF), F32),
            pltpu.VMEM((ROWS, HALF), BF16),
            pltpu.VMEM((ROWS, HALF), BF16),
            pltpu.VMEM((2, ROWS // 2, ALL // 2), BF16),
            pltpu.VMEM((2, ROWS, ALL), BF16),
            pltpu.VMEM((2, ALL, ROWS), BF16),
            pltpu.VMEM((2, ALL, ROWS), BF16),
            pltpu.VMEM((NZ, TOK, WIDE[0]), F32),
            pltpu.VMEM((NZ, TOK, WIDE[1]), F32),
            pltpu.VMEM((*both, NZ - 1, TOK, WIDE[1]), BF16),
            pltpu.VMEM((*both, NZ - 1, TOK, WIDE[1]), BF16),
            dma((3,)),
            dma(hops),
            dma(hops),
            dma((2, *both, *hops)),
            dma((2, *both, *hops)),
        ]
        + [dma(both)] * 2
        + [dma((2, *both))] * 2
        + [dma(both)] * 4
        + [dma((*both, *hops))] * 2
        + [dma] * 2
        + [pltpu.SemaphoreType.REGULAR],
        compiler_params=pltpu.CompilerParams(
            collective_id=0, has_side_effects=True, vmem_limit_bytes=63 * 2**20
        ),
    )(
        og,
        cg,
        xin[0],
        jnp.transpose(ids[0], (2, 0, 1)),
        jnp.transpose(prob[0], (2, 0, 1)),
        gate_weight[0, 0].T,
        up_weight[0, 0].T,
        down_weight[0, 0],
    )
    return out[None], jnp.transpose(gate, (1, 2, 0))[None]


def solution(mesh):
    rows = ("group", "local")
    return jax.shard_map(
        local,
        mesh=mesh,
        in_specs=(
            P(None, rows, None),
            P(rows, None),
            P("pipe", None, rows, None),
            P("pipe", None, rows, None),
            P("pipe", None, rows, None),
            P("pipe", rows, None, None),
            P("pipe", rows, None, None),
            P("pipe", rows, None, None),
        ),
        out_specs=(P("pipe", None, rows, None), P("pipe", None, rows, None)),
        check_vma=False,
    )
```

```python
import functools

import jax
import jax.numpy as jnp
from jax import lax
from jax.experimental import pallas as pl
from jax.experimental.pallas import tpu as pltpu
from jax.sharding import PartitionSpec as P

MESH = pl.DeviceIdType.MESH
NX, NY, NZ = 4, 4, 8
NG = NX * NY
TOK, D, HALF, SLOTS = 32, 2048, 704, 4
ROWS = NG * TOK
ALL = NZ * TOK
HALVES = 2
W = D // HALVES
EXTRA = 128
WIDE = (W, W + EXTRA)
STEPS = ((4, 3), (3, 4))
NT = (((1,), (1,)), ((), ()))
F32, BF16 = jnp.float32, jnp.bfloat16


def nt_dot(a, b):
    return lax.dot_general(a, b, NT, preferred_element_type=F32)


def kernel(
    og_ref, cg_ref, xin_ref, ids_ref, pr_ref, wg_hbm, wu_hbm, wd_hbm,
    out_ref, gate_ref,
    wg, wu, wd, meta, own_grad, passed, finished,
    gathered, x_picked, x_arrived, g_picked, g_arrived,
    back0, back1, came0, came1,
    a_acc, b_acc, q_acc, da_buf, db_buf, xmat, dmat, cmat, mmat, p0, p1, rs_send, rs_recv,
    w_sem, meta_ss, meta_rs, ag_ss, ag_rs, x_ss, x_rs, f_ss, f_rs, g_ss, g_rs,
    r_ss, r_rs, rs_ss, rs_rs, pass_ss, pass_rs, turn,
):
    pipe = lax.axis_index("pipe")
    g = lax.axis_index("group")
    z = lax.axis_index("local")
    x, y = g // NY, g % NY
    side = z % 2
    base = z - side
    expert = 4 * g + z // 2
    up = (pipe, g, lax.rem(z + 1, NZ))
    down = (pipe, g, lax.rem(z + NZ - 1, NZ))
    mate = (pipe, g, z + 1 - 2 * side)
    partner = (1 - pipe, g, z)
    back, came, sums = (back0, back1), (came0, came1), (p0, p1)
    is_even, is_odd = side == 0, side == 1
    first, last = pipe == 0, pipe == 1
    top = ids_ref.shape[0]

    def remote(src, dst, ss, rs, device):
        return pltpu.make_async_remote_copy(
            src_ref=src, dst_ref=dst, send_sem=ss, recv_sem=rs, device_id=device, device_id_type=MESH
        )

    loads = []
    for i, (h, v) in enumerate(((wg_hbm, wg), (wu_hbm, wu), (wd_hbm, wd))):
        load = pltpu.make_async_copy(h, v, w_sem.at[i])
        loads.append(load)

    barrier = pltpu.get_barrier_semaphore()

    def plane_peer(i):
        dx = i % NX
        dy = lax.rem(i // NX - dx + NY, NY)
        return lax.rem(x + dx, NX) * NY + lax.rem(y + dy, NY)

    def greet(i, carry):
        pl.semaphore_signal(barrier, inc=1, device_id=(pipe, plane_peer(i), z), device_id_type=MESH)
        return carry

    for device in (up, down, partner):
        pl.semaphore_signal(barrier, inc=1, device_id=device, device_id_type=MESH)
    lax.fori_loop(1, NG, greet, 0)

    lane = lax.broadcasted_iota(jnp.int32, (TOK, EXTRA), 1)
    i0 = lax.broadcasted_iota(jnp.int32, (TOK, TOK), 0)
    i1 = lax.broadcasted_iota(jnp.int32, (TOK, TOK), 1)
    lower = (i0 > i1).astype(BF16)
    same = (i0 == i1).astype(BF16)

    def columns(ref, m):
        rows = jnp.concatenate([ref[k, pl.ds(m, 1), :].astype(F32) for k in range(top)], axis=0)
        return nt_dot(same, rows.astype(BF16))

    ids = [columns(ids_ref, m).astype(jnp.int32) for m in range(2)]
    for m in range(2):
        probs = columns(pr_ref, m)
        chosen = jnp.zeros((TOK, EXTRA), F32)
        weight = jnp.zeros((TOK, EXTRA), F32)
        for k in range(top):
            chosen += (lane == ids[m][:, k : k + 1]).astype(F32)
            weight += jnp.where(lane == ids[m][:, k : k + 1] + 64, probs[:, k : k + 1], 0.0)
        before = jnp.dot(lower, chosen.astype(BF16), preferred_element_type=F32)
        meta[z, m] = (chosen * (before + 1.0) + weight).astype(BF16)
    own_grad[0] = jnp.where(last, og_ref[0].astype(F32), cg_ref[...].astype(F32)).astype(BF16)

    def place_own(kind, m):
        src = xin_ref[m] if kind == 0 else own_grad[m]
        for c in range(HALVES):
            gathered[kind, m, c, z] = src[:, c * W : (c + 1) * W]

    place_own(0, 0)
    place_own(1, 0)
    place_own(0, 1)
    pl.semaphore_wait(barrier, NG - 1 + 3)

    def run(items, hooks=None, ahead=0, keys=(0, 1, 2, 3), pace=(2,) * 5):
        order = sorted(
            (keys[i] + pace[i] * s if s or i >= ahead else i - NZ, i, s)
            for i, (_, n, _) in enumerate(items)
            for s in range(n)
        )
        for _, i, s in order:
            items[i][0](s)
            if hooks and s == items[i][1] - 1:
                hooks[i]()

    def ring(own, at, ss, rs, counts):
        nr, nl = counts

        def hop(direction, s):
            if direction == 0:
                origin, device, slot = lax.rem(z - s + NZ, NZ), up, s
            else:
                origin, device, slot = lax.rem(z + s, NZ), down, nr + s
            return remote(own if s == 0 else at(origin), at(origin), ss.at[slot], rs.at[slot], device)

        def step(s):
            for direction, count in ((0, nr), (1, nl)):
                if s >= 1 and s - 1 < count:
                    hop(direction, s - 1).wait_recv()
                if s < count:
                    hop(direction, s).start()

        def close():
            for direction, count in ((0, nr), (1, nl)):
                for s in range(count):
                    hop(direction, s).wait_send()

        return step, max(nr, nl) + 1, close

    def half_ring(own, at, ss, rs):
        def hop(direction, s):
            if direction == 0:
                origin, device, slot = lax.rem(z - s + NZ, NZ), up, s
            else:
                origin, device, slot = lax.rem(z + s, NZ), down, 3 + s
            return remote(own if s == 0 else at(origin), at(origin), ss.at[slot], rs.at[slot], device)

        def step(s):
            for direction in range(2):
                sends, takes = (is_odd, is_even) if direction == 0 else (is_even, is_odd)
                if s in (1, 2):
                    hop(direction, s - 1).wait_recv()
                if s == 3:
                    pl.when(takes)(lambda: hop(direction, 2).wait_recv())
                if s < 2:
                    hop(direction, s).start()
                if s == 2:
                    pl.when(sends)(lambda: hop(direction, 2).start())

        def close():
            for direction in range(2):
                for s in range(2):
                    hop(direction, s).wait_send()
                pl.when(is_odd if direction == 0 else is_even)(lambda: hop(direction, 2).wait_send())

        return step, 4, close

    def gather(kind, m, c, whole):
        src = (xin_ref if kind == 0 else own_grad).at[m, :, pl.ds(c * W, W)]
        at = lambda o: gathered.at[kind, m, c, o]
        ss, rs = ag_ss.at[kind, m, c], ag_rs.at[kind, m, c]
        return ring(src, at, ss, rs, STEPS[c]) if whole else half_ring(src, at, ss, rs)

    def fan_out(src, dst, ss, rs):
        def send(i, carry):
            peer = plane_peer(i)
            remote(src(peer), dst(g), ss, rs, (pipe, peer, z)).start()
            return carry

        lax.fori_loop(1, NG, send, 0)

    def drain(ref, sem):
        pltpu.make_async_copy(ref, ref, sem).wait()

    def origin_of(order):
        return lax.rem(base - 3 + NZ + order, NZ)

    def iota(shape, dim):
        return lax.broadcasted_iota(jnp.int32, shape, dim)

    def build_x_maps():
        hr = TOK // 2
        sel = (iota((NG * hr, EXTRA), 1) == iota((NG * hr, EXTRA), 0) // hr * 4 + z // 2).astype(BF16)
        r, t = iota((NG * hr, ALL // 2), 0), iota((NG * hr, ALL // 2), 1)
        want = jnp.where(r % hr // SLOTS == t // TOK, r % SLOTS + 1, -1).astype(F32)
        for m in range(2):
            near = jnp.concatenate([meta[origin_of(4 * side + j), m] for j in range(4)], axis=0)
            xmat[m] = (nt_dot(sel, near) == want).astype(BF16)

    def build_maps():
        e_lane = iota((ROWS, EXTRA), 1)
        e_row = iota((ROWS, EXTRA), 0) // TOK * 4 + z // 2
        sel_slot = (e_lane == e_row).astype(BF16)
        sel_prob = (e_lane == e_row + 64).astype(BF16)
        r, t = iota((ROWS, ALL), 0), iota((ROWS, ALL), 1)
        want0 = jnp.where(origin_of(r % TOK // SLOTS) == t // TOK, r % SLOTS + 1, -1).astype(F32)
        r, t = iota((ALL, ROWS), 1), iota((ALL, ROWS), 0)
        want1 = jnp.where(origin_of(r % TOK // SLOTS) == t // TOK, r % SLOTS + 1, -1).astype(F32)
        for m in range(2):
            table = meta[:, m].reshape(ALL, EXTRA)
            dmat[m] = (nt_dot(sel_slot, table) == want0).astype(BF16)
            hit = nt_dot(table, sel_slot) == want1
            mmat[m] = hit.astype(BF16)
            cmat[m] = jnp.where(hit, nt_dot(table, sel_prob), 0.0).astype(BF16)

    my_half = pl.ds(pl.multiple_of(side * (TOK // 2), TOK // 2), TOK // 2)

    route = ((x_picked, x_arrived, x_ss, x_rs), (g_picked, g_arrived, g_ss, g_rs))

    def dispatch(kind, m, c):
        picked, arrived, ss, rs = route[kind]
        tokens = gathered[kind, m, c].reshape(ALL, W)
        rows = jnp.dot(dmat[m], tokens, preferred_element_type=F32).astype(BF16)
        picked[m, c] = rows.reshape(NG, TOK, W)
        fan_out(
            lambda peer: picked.at[m, c, peer], lambda col: arrived.at[m, c, col], ss.at[m, c], rs.at[m, c]
        )
        arrived[m, c, g] = picked[m, c, g]

    def dispatch_half(kind, m, c):
        picked, arrived, ss, rs = route[kind]
        tokens = jnp.concatenate([gathered[kind, m, c, origin_of(4 * side + j)] for j in range(4)], axis=0)
        rows = jnp.dot(xmat[m], tokens, preferred_element_type=F32).astype(BF16)
        picked[m, c, :, : TOK // 2, :] = rows.reshape(NG, TOK // 2, W)
        fan_out(
            lambda peer: picked.at[m, c, peer, pl.ds(0, TOK // 2), :],
            lambda col: arrived.at[m, c, col, my_half, :],
            ss.at[m, c],
            rs.at[m, c],
        )
        arrived[m, c, g, my_half, :] = picked[m, c, g, : TOK // 2, :]

    def halves(kind, m, c):
        return route[kind][0].at[m, c, pl.ds(0, NG - 1), pl.ds(0, TOK // 2), :]

    def exchange(kind, m, c, at, count):
        block = route[kind][1].at[m, c, pl.ds(at, count), my_half, :]
        return remote(block, block, f_ss.at[kind, m, c], f_rs.at[kind, m, c], mate)

    def forward(kind, m, c):
        drain(halves(kind, m, c), route[kind][3].at[m, c])
        for part in range(4):
            exchange(kind, m, c, part * NG // 4, NG // 4).start()

    def project(rows_ref, c, pairs):
        rows = rows_ref[...].reshape(ROWS, W)
        for weight, acc in pairs:
            value = nt_dot(rows, weight[:, c * W : (c + 1) * W])
            acc[...] = value if c == 0 else acc[...] + value

    def project_x(m, c):
        exchange(0, m, c, 0, NG).wait_recv()
        project(x_arrived.at[m, c], c, ((wg, a_acc), (wu, b_acc)))

    def project_g(m, c, whole):
        if whole:
            drain(g_arrived.at[m, c, pl.ds(0, NG - 1)], g_rs.at[m, c])
        else:
            exchange(1, m, c, 0, NG).wait_recv()
        project(g_arrived.at[m, c], c, ((wd, q_acc),))

    def activate(m):
        step_rows = 128
        gate_lane = iota((step_rows, EXTRA), 1)

        def part(i, carry):
            at = pl.ds(pl.multiple_of(i * step_rows, step_rows), step_rows)
            a, b, q = a_acc[at, :], b_acc[at, :], q_acc[at, :]
            sig = 0.5 * jnp.tanh(0.5 * a) + 0.5
            silu = a * sig
            qs = q * silu
            gate = jnp.sum(qs * b, axis=1, keepdims=True)
            da_buf[at, :] = (q * b * sig * (1.0 + a * (1.0 - sig))).astype(BF16)
            db_buf[at, :] = qs.astype(BF16)
            extra = jnp.where(gate_lane == expert, gate, 0.0).astype(BF16)
            n = step_rows // TOK
            back1[m, pl.ds(i * n, n), :, W:] = extra.reshape(n, TOK, EXTRA)
            return carry

        lax.fori_loop(0, ROWS // step_rows, part, 0)

    def backward(m, c):
        cols = slice(c * W, (c + 1) * W)
        u = jnp.dot(da_buf[...], wg[:, cols], preferred_element_type=F32)
        u = u + jnp.dot(db_buf[...], wu[:, cols], preferred_element_type=F32)
        back[c][m, :, :, :W] = u.astype(BF16).reshape(NG, TOK, W)

    def send_back(m, c):
        fan_out(
            lambda peer: back[c].at[m, peer], lambda col: came[c].at[m, col], r_ss.at[m, c], r_rs.at[m, c]
        )
        came[c][m, g] = back[c][m, g]

    def combine(m, c):
        drain(came[c].at[m, pl.ds(0, NG - 1)], r_rs.at[m, c])
        rows = came[c][m].reshape(ROWS, WIDE[c])
        value = jnp.dot(cmat[m], rows[:, :W], preferred_element_type=F32)
        sums[c][m, :, :, :W] = value.reshape(NZ, TOK, W)
        if c == 1:
            extra = jnp.dot(mmat[m], rows[:, W:], preferred_element_type=F32)
            sums[c][m, :, :, W:] = extra.reshape(NZ, TOK, EXTRA)

    def scatter(m, c):
        nr, nl = STEPS[c]
        width = WIDE[c]

        def buf(ref, slot):
            return ref.at[m, c, slot, :, pl.ds(0, width)]

        def hop(direction, s):
            slot, device = (s, up) if direction == 0 else (nr + s, down)
            return remote(
                buf(rs_send, slot), buf(rs_recv, slot), rs_ss.at[m, c, slot], rs_rs.at[m, c, slot], device
            )

        def step(s):
            for direction, count in ((0, nr), (1, nl)):
                if s >= 1 and s - 1 < count:
                    hop(direction, s - 1).wait_recv()
                if s < count:
                    slot = s if direction == 0 else nr + s
                    dest = lax.rem(z + nr - s, NZ) if direction == 0 else lax.rem(z - nl + s + NZ, NZ)
                    value = sums[c][m, dest]
                    if s >= 1:
                        value = value + rs_recv[m, c, slot - 1, :, :width].astype(F32)
                    rs_send[m, c, slot, :, :width] = value.astype(BF16)
                    hop(direction, s).start()

        def close():
            for direction, count in ((0, nr), (1, nl)):
                for s in range(count):
                    hop(direction, s).wait_send()

        return step, max(nr, nl) + 1, close

    def finish(m):
        for c in range(HALVES):
            nr, nl = STEPS[c]
            width = WIDE[c]
            total = sums[c][m, z]
            total += rs_recv[m, c, nr - 1, :, :width].astype(F32)
            total += rs_recv[m, c, nr + nl - 1, :, :width].astype(F32)
            cols = slice(c * W, (c + 1) * W)
            value = (own_grad[m, :, cols].astype(F32) + total[:, :W]).astype(BF16)
            out_ref[m, :, cols] = value
            if m == 0:
                finished[:, cols] = value
            if c == 1:
                extra = total[:, W:]
                gates = jnp.zeros((TOK, EXTRA), F32)
                for k in range(top):
                    picked = jnp.sum(jnp.where(lane == ids[m][:, k : k + 1], extra, 0.0), axis=1, keepdims=True)
                    gates += jnp.where(lane == k, picked, 0.0)
                flat = lax.dot_general(
                    gates.astype(BF16), same, (((0,), (0,)), ((), ())), preferred_element_type=F32
                ).astype(BF16)
                for k in range(top):
                    gate_ref[k, pl.ds(m, 1), :] = flat[k : k + 1, :]

    def collect(m, between=lambda: None):
        for c in range(HALVES):
            combine(m, c)
        between()
        run([scatter(m, c) for c in range(HALVES)])
        finish(m)

    both = range(HALVES)
    handed = lambda: remote(finished, passed, pass_ss, pass_rs, partner)
    second_x = [gather(0, 1, c, False) for c in both]
    half_g = [gather(1, 1, c, False) for c in both]
    whole_g = [gather(1, 1, c, True) for c in both]
    send_x = [lambda c=c: dispatch_half(0, 1, c) for c in both]
    send_half_g = [lambda c=c: dispatch_half(1, 1, c) for c in both]
    send_whole_g = [lambda c=c: dispatch(1, 1, c) for c in both]

    def release():
        pl.semaphore_signal(turn, inc=1, device_id=partner, device_id_type=MESH)

    items = [ring(meta.at[z], lambda o: meta.at[o], meta_ss, meta_rs, STEPS[0])]
    items += [gather(kind, 0, c, kind == 1) for kind in range(2) for c in both]

    def rest_of_x():
        dispatch_half(0, 0, 1)
        build_maps()

    hooks = [build_x_maps, lambda: dispatch_half(0, 0, 0), rest_of_x]
    hooks += [lambda c=c: dispatch(1, 0, c) for c in both]
    run(items, hooks, 3, (-1, 0, 0.5, 3, 4), (1.4, 2, 2, 2, 2))

    for load in loads:
        load.start()

    @pl.when(first)
    def _():
        run(second_x, send_x)

    for c in both:
        forward(0, 0, c)
    for load in loads:
        load.wait()
    for c in both:
        project_x(0, c)
    for c in both:
        project_g(0, c, True)

    @pl.when(first)
    def _():
        for c in both:
            forward(0, 1, c)

    activate(0)
    for c in both:
        backward(0, c)
        pl.when(last)(lambda: send_back(0, c))

    @pl.when(last)
    def _():
        own_grad[1] = og_ref[1]
        place_own(1, 1)
        run(second_x + whole_g, send_x + send_whole_g)
        collect(0, release)
        handed().start()
        for c in both:
            forward(0, 1, c)
        for c in both:
            project_g(1, c, True)
        for c in both:
            project_x(1, c)
        handed().wait_send()

    @pl.when(first)
    def _():
        pl.semaphore_wait(turn, 1)
        for c in both:
            send_back(0, c)
        handed().wait_recv()
        own_grad[1] = passed[...]
        place_own(1, 1)
        run(half_g, send_half_g)
        for c in both:
            forward(1, 1, c)
        for c in both:
            project_x(1, c)
        for c in both:
            project_g(1, c, False)

    activate(1)
    for c in both:
        backward(1, c)
        send_back(1, c)

    @pl.when(first)
    def _():
        for c in both:
            combine(0, c)
        hops = [[scatter(m, c) for c in both] for m in range(2)]
        for s in range(3):
            for hop in hops[0]:
                hop[0](s)
        for c in both:
            combine(1, c)
        for s in range(5):
            for hop in hops[1]:
                hop[0](s)
            if s < 2:
                for hop in hops[0]:
                    hop[0](s + 3)
            if s == 2:
                finish(0)
        finish(1)

    @pl.when(last)
    def _():
        collect(1)

    for item in items + second_x + [scatter(m, c) for m in range(2) for c in both]:
        item[2]()
    for c in both:
        for m in range(2):
            exchange(0, m, c, 0, NG).wait_send()
            drain(halves(0, m, c), x_ss.at[m, c])
            drain(back[c].at[m, pl.ds(0, NG - 1)], r_ss.at[m, c])
        drain(g_picked.at[0, c, pl.ds(0, NG - 1)], g_ss.at[0, c])

    @pl.when(first)
    def _():
        for c in both:
            half_g[c][2]()
            exchange(1, 1, c, 0, NG).wait_send()
            drain(halves(1, 1, c), g_ss.at[1, c])

    @pl.when(last)
    def _():
        for c in both:
            whole_g[c][2]()
            drain(g_picked.at[1, c, pl.ds(0, NG - 1)], g_ss.at[1, c])


def local(og, cg, xin, ids, prob, gate_weight, up_weight, down_weight):
    vmem = pl.BlockSpec(memory_space=pltpu.VMEM)
    hbm = pl.BlockSpec(memory_space=pl.ANY)
    dma = pltpu.SemaphoreType.DMA
    top = ids.shape[-1]
    both = (2, HALVES)
    hops = (NZ - 1,)
    out, gate = pl.pallas_call(
        kernel,
        out_shape=(
            jax.ShapeDtypeStruct((2, TOK, D), BF16),
            jax.ShapeDtypeStruct((top, 2, TOK), BF16),
        ),
        in_specs=[vmem] * 5 + [hbm] * 3,
        out_specs=(vmem, vmem),
        scratch_shapes=[
            pltpu.VMEM((HALF, D), BF16),
            pltpu.VMEM((HALF, D), BF16),
            pltpu.VMEM((HALF, D), BF16),
            pltpu.VMEM((NZ, 2, TOK, EXTRA), BF16),
            pltpu.VMEM((2, TOK, D), BF16),
            pltpu.VMEM((TOK, D), BF16),
            pltpu.VMEM((TOK, D), BF16),
            pltpu.VMEM((2, *both, NZ, TOK, W), BF16),
            pltpu.VMEM((*both, NG, TOK, W), BF16),
            pltpu.VMEM((*both, NG, TOK, W), BF16),
            pltpu.VMEM((*both, NG, TOK, W), BF16),
            pltpu.VMEM((*both, NG, TOK, W), BF16),
            pltpu.VMEM((2, NG, TOK, WIDE[0]), BF16),
            pltpu.VMEM((2, NG, TOK, WIDE[1]), BF16),
            pltpu.VMEM((2, NG, TOK, WIDE[0]), BF16),
            pltpu.VMEM((2, NG, TOK, WIDE[1]), BF16),
            pltpu.VMEM((ROWS, HALF), F32),
            pltpu.VMEM((ROWS, HALF), F32),
            pltpu.VMEM((ROWS, HALF), F32),
            pltpu.VMEM((ROWS, HALF), BF16),
            pltpu.VMEM((ROWS, HALF), BF16),
            pltpu.VMEM((2, ROWS // 2, ALL // 2), BF16),
            pltpu.VMEM((2, ROWS, ALL), BF16),
            pltpu.VMEM((2, ALL, ROWS), BF16),
            pltpu.VMEM((2, ALL, ROWS), BF16),
            pltpu.VMEM((2, NZ, TOK, WIDE[0]), F32),
            pltpu.VMEM((2, NZ, TOK, WIDE[1]), F32),
            pltpu.VMEM((*both, NZ - 1, TOK, WIDE[1]), BF16),
            pltpu.VMEM((*both, NZ - 1, TOK, WIDE[1]), BF16),
            dma((3,)),
            dma(hops),
            dma(hops),
            dma((2, *both, *hops)),
            dma((2, *both, *hops)),
        ]
        + [dma(both)] * 2
        + [dma((2, *both))] * 2
        + [dma(both)] * 4
        + [dma((*both, *hops))] * 2
        + [dma] * 2
        + [pltpu.SemaphoreType.REGULAR],
        compiler_params=pltpu.CompilerParams(
            collective_id=0, has_side_effects=True, vmem_limit_bytes=63 * 2**20
        ),
    )(
        og,
        cg,
        xin[0],
        jnp.transpose(ids[0], (2, 0, 1)),
        jnp.transpose(prob[0], (2, 0, 1)),
        gate_weight[0, 0].T,
        up_weight[0, 0].T,
        down_weight[0, 0],
    )
    return out[None], jnp.transpose(gate, (1, 2, 0))[None]


def solution(mesh):
    rows = ("group", "local")
    return jax.shard_map(
        local,
        mesh=mesh,
        in_specs=(
            P(None, rows, None),
            P(rows, None),
            P("pipe", None, rows, None),
            P("pipe", None, rows, None),
            P("pipe", None, rows, None),
            P("pipe", rows, None, None),
            P("pipe", rows, None, None),
            P("pipe", rows, None, None),
        ),
        out_specs=(P("pipe", None, rows, None), P("pipe", None, rows, None)),
        check_vma=False,
    )
```
